128 devices in a mesh: clu: 8 (over z, y_lo), ang: 16 (over y_hi, x, core).
Axes of the slice: x: 4, y: 4 (y_hi: 2, y_lo: 2; y = y_hi * 2 + y_lo), z: 4, core: 2. Of those that a mesh axis runs over, the one named last changes fastest.
Arguments:
- patterns7: bfloat16 [32768, 2, 64, 128], P(('clu', 'ang')), may hold values from -6 to 6
- polar_up7: bfloat16 [128, 64], replicated, may hold values from -0.25 to 0.25
- azimuth_up7: bfloat16 [128, 256], replicated, may hold values from -0.5 to 0.5
- polar_up6: bfloat16 [256, 128], replicated, may hold values from -0.1875 to 0.1875
- azimuth_up6: bfloat16 [256, 512], replicated, may hold values from -0.375 to 0.375
- polar_first: int32 [512], replicated, may hold values from 0 to 252, as said below
- polar_weights: bfloat16 [512, 4], replicated, may hold values from -1 to 1
- azimuth_first: int32 [1024], replicated, may hold values from 0 to 511, as said below
- azimuth_weights: bfloat16 [1024, 4], replicated, may hold values from -3 to 3
- transfer5: bfloat16 [316, 2, 256, 512], P(None, None, 'ang', 'clu'), may hold values from -1.5 to 1.5
- sources5: int32 [512, 16], replicated, may hold values from -1 to 511, as said below
- offsets5: int32 [512, 16], replicated, may hold values from -1 to 315, as said below
- transfer4: bfloat16 [316, 2, 512, 1024], P(None, None, 'ang', 'clu'), may hold values from -1.5 to 1.5
- sources4: int32 [64, 16], replicated, may hold values from -1 to 63, as said below
- offsets4: int32 [64, 16], replicated, may hold values from -1 to 315, as said below
Outputs:
- translated5: bfloat16 [512, 2, 256, 512], P(None, None, 'ang', 'clu')
- translated4: bfloat16 [64, 2, 512, 1024], P(None, None, 'ang', 'clu')
The draws below stay inside these ranges and needn't reach their ends.
Inputs may be any that keep to these rules, and one draw needn't show every extreme that they name: The theta stencil of target row r reads source rows polar_first[r] to polar_first[r] + 3, all within floor(r / 2) - 3 to floor(r / 2) + 3. The phi stencil of target column c reads source columns (azimuth_first[c] + k) mod 512, k = 0 to 3, all within floor(c / 2) - 3 to floor(c / 2) + 3 modulo 512. `sources5`: row t lists source clusters of target t: live entries first, then -1; never t itself; at least one live entry. `offsets5`: displacement id of each slot; -1 exactly where sources5 is -1. `sources4`: row t lists source clusters of target t: live entries first, then -1; never t itself; at least one live entry. `offsets4`: displacement id of each slot; -1 exactly where sources4 is -1.
All inputs are finite; a program needn't handle non-finite values.
Results may differ from the reference program's by a relative error of at most 0.015.
Values may be sent and summed in bfloat16 or wider, within the bound.
No kernel may reach another device: no remote copies, remote signals or barrier semaphores. Data moves between devices by JAX's collectives and lax.ppermute only.
A program may use at most 192 MiB of HBM per device.

```python
import math
import jax
import jax.numpy as jnp
from jax import lax

T4 = 512
F4 = 1024
LIST = 16
DISP = 316
T5 = 256
F5 = 512
T6 = 128
F6 = 256
T7 = 64
F7 = 128
NC7 = 32768
NC5 = 512
NC4 = 64


def draw_polar_first(key, part):
    target_rows = jnp.arange(T4, dtype=jnp.int32)
    jitter = jax.random.randint(key, (T4,), 0, 2, dtype=jnp.int32)
    return jnp.clip(target_rows // 2 - 1 + jitter, 0, T5 - 4)


def draw_azimuth_first(key, part):
    target_cols = jnp.arange(F4, dtype=jnp.int32)
    jitter = jax.random.randint(key, (F4,), 0, 2, dtype=jnp.int32)
    jitter = jnp.where(target_cols < 4, 0, jitter)
    return (target_cols // 2 - 1 + jitter) % F5


def interaction_lists(key, salt, targets):
    base_key = jax.random.fold_in(key, salt)
    key_source, key_offset, key_count = jax.random.split(base_key, 3)
    target_index = jnp.arange(targets, dtype=jnp.int32)[:, None]
    steps_away = jax.random.randint(key_source, (targets, LIST), 1, targets, dtype=jnp.int32)
    source_ids = (target_index + steps_away) % targets
    offset_ids = jax.random.randint(key_offset, (targets, LIST), 0, DISP, dtype=jnp.int32)
    live_count = jax.random.randint(key_count, (targets,), LIST // 2, LIST + 1, dtype=jnp.int32)
    live_count = live_count.at[0].set(LIST).at[1].set(LIST // 2)
    source_ids = source_ids.at[0, 0].set(targets - 1).at[1, 0].set(0)
    offset_ids = offset_ids.at[0, 0].set(DISP - 1).at[0, 1].set(0)
    live_mask = jnp.arange(LIST, dtype=jnp.int32)[None, :] < live_count[:, None]
    return (jnp.where(live_mask, source_ids, -1), jnp.where(live_mask, offset_ids, -1))


def draw_sources5(key, part):
    return interaction_lists(key, 5, NC5)[0]


def draw_offsets5(key, part):
    return interaction_lists(key, 5, NC5)[1]


def draw_sources4(key, part):
    return interaction_lists(key, 4, NC4)[0]


def draw_offsets4(key, part):
    return interaction_lists(key, 4, NC4)[1]


def block_levels(stream_key, shape, pieces, smallest, top_value):
    level = 1.0
    for axis_at, blocks in pieces:
        steps = jax.random.uniform(jax.random.fold_in(jax.random.fold_in(stream_key, 6), axis_at), (blocks,), jnp.float32, smallest / len(pieces), top_value / len(pieces))
        level = level * jnp.repeat(jnp.exp(steps), shape[axis_at] // blocks).reshape((-1,) + (1,) * (len(shape) - 1 - axis_at))
    return level


def bell_draw(stream_key, dims, spread, most, cuts=(), held_as=jnp.bfloat16):
    array = jax.random.normal(stream_key, dims, jnp.float32) * spread
    if len(cuts) > 0:
        array = block_levels(stream_key, dims, cuts, -0.22, 0.18) * array
    return jnp.clip(array, min=-most, max=most).astype(held_as)


def setup_inputs(seed: int = 0) -> dict:
    seeds = jax.random.split(jax.random.key(seed), 16)
    return {
        "patterns7": bell_draw(seeds[0], (NC7, 2, T7, F7), 1.0, 6.0, ((0, 128),)),
        "polar_up7": bell_draw(seeds[1], (T6, T7), (8 * T7) ** -0.5, 0.25),
        "azimuth_up7": bell_draw(seeds[2], (F7, F6), F7 ** -0.5, 0.5),
        "polar_up6": bell_draw(seeds[3], (T5, T6), (8 * T6) ** -0.5, 0.1875),
        "azimuth_up6": bell_draw(seeds[4], (F6, F5), F6 ** -0.5, 0.375),
        "polar_first": draw_polar_first(jax.random.fold_in(seeds[15], 71), 0),
        "polar_weights": bell_draw(seeds[6], (T4, 4), 32 ** -0.5, 1.0),
        "azimuth_first": draw_azimuth_first(jax.random.fold_in(seeds[15], 71), 0),
        "azimuth_weights": bell_draw(seeds[8], (F4, 4), 4 ** -0.5, 3.0),
        "transfer5": bell_draw(seeds[9], (DISP, 2, T5, F5), 0.25, 1.5, ((2, 16), (3, 8))),
        "sources5": draw_sources5(jax.random.fold_in(seeds[15], 71), 0),
        "offsets5": draw_offsets5(jax.random.fold_in(seeds[15], 71), 0),
        "transfer4": bell_draw(seeds[12], (DISP, 2, T4, F4), 0.25, 1.5, ((2, 16), (3, 8))),
        "sources4": draw_sources4(jax.random.fold_in(seeds[15], 71), 0),
        "offsets4": draw_offsets4(jax.random.fold_in(seeds[15], 71), 0),
    }


def octant_signs():
    octant = jnp.arange(8, dtype=jnp.int32)
    sign_first = (2 * (octant % 2) - 1).astype(jnp.float32)
    sign_second = (2 * ((octant // 2) % 2) - 1).astype(jnp.float32)
    sign_third = (2 * (octant // 4) - 1).astype(jnp.float32)
    return sign_first, sign_second, sign_third


def phase_tables(polar_index, azimuth_index, polar_count, azimuth_count):
    polar_angle = (polar_index + 0.5) * (math.pi / polar_count)
    azimuth_angle = azimuth_index * (2.0 * math.pi / azimuth_count)
    direction_x = jnp.sin(polar_angle)[:, None] * jnp.cos(azimuth_angle)[None, :]
    direction_y = jnp.sin(polar_angle)[:, None] * jnp.sin(azimuth_angle)[None, :]
    direction_z = jnp.cos(polar_angle)[:, None] * jnp.ones_like(azimuth_angle)[None, :]
    sign_first, sign_second, sign_third = octant_signs()
    phase_angle = (polar_count / 8.0) * (sign_first[:, None, None] * direction_x + sign_second[:, None, None] * direction_y + sign_third[:, None, None] * direction_z)
    return jnp.cos(phase_angle), jnp.sin(phase_angle)


def shift_sum(child_terms, cosine, sine):
    real_part = jnp.sum(child_terms[:, :, 0] * cosine - child_terms[:, :, 1] * sine, axis=1)
    imag_part = jnp.sum(child_terms[:, :, 0] * sine + child_terms[:, :, 1] * cosine, axis=1)
    return jnp.stack([real_part, imag_part], axis=1).astype(jnp.bfloat16)


def stencil_matrix(tap_index, weights, column_count):
    matches = (tap_index[:, :, None] == jnp.arange(column_count, dtype=jnp.int32)[None, None, :]).astype(jnp.float32)
    return jnp.sum(weights.astype(jnp.float32)[:, :, None] * matches, axis=1)


def parent_block(children, polar_matrix, azimuth_matrix, cosine, sine):
    parents = children.shape[0] // 8
    grouped = children.reshape(parents, 8, 2, children.shape[2], children.shape[3]).astype(jnp.float32)
    halfway = jnp.einsum("ut,pkcts->pkcus", polar_matrix.astype(jnp.float32), grouped).astype(jnp.bfloat16)
    halfway = lax.optimization_barrier(halfway).astype(jnp.float32)
    child_terms = jnp.einsum("pkcus,sv->pkcuv", halfway, azimuth_matrix.astype(jnp.float32))
    return shift_sum(child_terms, cosine, sine)


def aggregate(children, polar_matrix, azimuth_matrix, cosine, sine, block_parents):
    parent_total = children.shape[0] // 8
    group_size = math.gcd(parent_total, block_parents)
    blocks = children.reshape(parent_total // group_size, group_size * 8, 2, children.shape[2], children.shape[3])

    def one_block(block_piece):
        return parent_block(block_piece, polar_matrix, azimuth_matrix, cosine, sine)

    merged = lax.map(one_block, blocks)
    return merged.reshape(parent_total, 2, polar_matrix.shape[0], azimuth_matrix.shape[1])


def translate(patterns, transfer_table, sources, displacements, block_targets):
    targets = patterns.shape[0]
    group_size = math.gcd(targets, block_targets)
    flat_patterns = patterns.reshape(targets, 2, -1)
    flat_table = transfer_table.reshape(transfer_table.shape[0], 2, -1)

    def one_block(pair):
        source_block, offset_block = pair
        live_mask = (source_block >= 0).astype(jnp.float32)[:, :, None]
        picked = jnp.take(flat_patterns, jnp.maximum(source_block, 0), axis=0).astype(jnp.float32)
        factor = jnp.take(flat_table, jnp.maximum(offset_block, 0), axis=0).astype(jnp.float32)
        real_part = jnp.sum(live_mask * (factor[:, :, 0] * picked[:, :, 0] - factor[:, :, 1] * picked[:, :, 1]), axis=1)
        imag_part = jnp.sum(live_mask * (factor[:, :, 0] * picked[:, :, 1] + factor[:, :, 1] * picked[:, :, 0]), axis=1)
        return jnp.stack([real_part, imag_part], axis=1).astype(jnp.bfloat16)

    slots = sources.shape[1]
    merged = lax.map(one_block, (sources.reshape(targets // group_size, group_size, slots), displacements.reshape(targets // group_size, group_size, slots)))
    return merged.reshape(patterns.shape)


def reference(patterns7, polar_up7, azimuth_up7, polar_up6, azimuth_up6, polar_first, polar_weights, azimuth_first, azimuth_weights, transfer5, sources5, offsets5, transfer4, sources4, offsets4):
    cosine6, sine6 = phase_tables(jnp.arange(T6, dtype=jnp.float32), jnp.arange(F6, dtype=jnp.float32), T6, F6)
    level6 = aggregate(patterns7, polar_up7, azimuth_up7, cosine6, sine6, 64)
    cosine5, sine5 = phase_tables(jnp.arange(T5, dtype=jnp.float32), jnp.arange(F5, dtype=jnp.float32), T5, F5)
    level5 = aggregate(level6, polar_up6, azimuth_up6, cosine5, sine5, 8)
    translated5 = translate(level5, transfer5, sources5, offsets5, 4)
    four_taps = jnp.arange(4, dtype=jnp.int32)[None, :]
    polar_matrix = stencil_matrix(polar_first[:, None] + four_taps, polar_weights, T5)
    azimuth_matrix = stencil_matrix((azimuth_first[:, None] + four_taps) % F5, azimuth_weights, F5).T
    cosine4, sine4 = phase_tables(jnp.arange(T4, dtype=jnp.float32), jnp.arange(F4, dtype=jnp.float32), T4, F4)
    level4 = aggregate(level5, polar_matrix, azimuth_matrix, cosine4, sine4, 2)
    translated4 = translate(level4, transfer4, sources4, offsets4, 1)
    return translated5, translated4
```

```python
import math

import jax
import jax.numpy as jnp
import numpy as np
from jax import lax
from jax.experimental import pallas as pl
from jax.experimental.pallas import tpu as pltpu
from jax.sharding import PartitionSpec as P

F32 = jnp.float32
BF16 = jnp.bfloat16
VMEM_LIMIT = 60 * 1024 * 1024


PAIRS = ((3, 0), (1, 2))


def theta_phase(rows):
    return rows / 8.0 * np.cos(np.pi * (np.arange(rows) + 0.5) / rows)


def plane_phases(rows, cols, count):
    theta = np.pi * (np.arange(rows) + 0.5) / rows
    phi = 2.0 * np.pi * np.arange(count) / cols
    x = np.sin(theta)[:, None] * np.cos(phi)[None, :]
    y = np.sin(theta)[:, None] * np.sin(phi)[None, :]
    return rows / 8.0 * (x + y), rows / 8.0 * (x - y)


def fold_factors(rows, inner):
    phase = theta_phase(rows)[:, None]
    cosine = np.broadcast_to(np.cos(phase), (rows, inner))
    sine = np.broadcast_to(np.sin(phase), (rows, inner))
    top = np.concatenate([cosine, sine, cosine, -sine], axis=1)
    bottom = np.concatenate([-sine, cosine, sine, cosine], axis=1)
    return top.astype(np.float32), bottom.astype(np.float32)


def dot(a, b):
    return jnp.dot(a, b, preferred_element_type=F32)


def dot_t(a, b):
    return lax.dot_general(a, b, (((1,), (1,)), ((), ())), preferred_element_type=F32)


def aggregate_body(
    pat, a7, b7, a6, b6, top7, bottom7, cz, sz, tab6, tab5, out, m7, m6, level6, mixed, half6
):
    rows7, rows6, rows5 = a7.shape[1], a7.shape[0], a6.shape[0]
    cols6, cols5 = b7.shape[1], b6.shape[1]

    @pl.when(pl.program_id(0) == 0)
    def _():
        src = lax.broadcasted_iota(jnp.int32, (rows7, 4 * rows7), 0)
        dst = lax.broadcasted_iota(jnp.int32, (rows7, 4 * rows7), 1)
        spread = jnp.where((dst & (rows7 - 1)) == src, 1.0, 0.0).astype(BF16)
        wide = dot(a7[...], spread)
        m7[0:rows6, :] = (wide * top7[...]).astype(BF16)
        m7[rows6 : 2 * rows6, :] = (wide * bottom7[...]).astype(BF16)
        base = a6[...].astype(F32)
        c = base * cz[...]
        s = base * sz[...]
        m6[0, :, 0:rows6] = c.astype(BF16)
        m6[0, :, rows6 : 2 * rows6] = (-s).astype(BF16)
        m6[1, :, 0:rows6] = c.astype(BF16)
        m6[1, :, rows6 : 2 * rows6] = s.astype(BF16)

    step = 2 * rows7
    for o6 in range(8):
        base = o6 * 8 * step
        parts = []
        for k in range(4):
            low = pat[base + k * step : base + (k + 1) * step, :]
            high = pat[base + (k + 4) * step : base + (k + 5) * step, :]
            parts.append(jnp.concatenate([low, high], axis=0))
        lanes = parts[0].shape[1]
        h = dot(m7[...], jnp.concatenate(parts, axis=1))
        rows = []
        for a, b in PAIRS:
            ya = h[:, a * lanes : (a + 1) * lanes]
            yb = h[:, b * lanes : (b + 1) * lanes]
            rows.append((ya + yb).astype(BF16))
            rows.append((ya - yb).astype(BF16))
        y = dot(jnp.concatenate(rows, axis=0), b7[...])
        for half in range(2):
            cols = slice(half * (cols6 // 2), (half + 1) * (cols6 // 2))
            re = None
            for q in range(2):
                at = q * 4 * rows6
                pr = y[at : at + rows6, cols]
                pi = y[at + rows6 : at + 2 * rows6, cols]
                qr = y[at + 2 * rows6 : at + 3 * rows6, cols]
                qi = y[at + 3 * rows6 : at + 4 * rows6, cols]
                c = tab6[2 * q]
                s = tab6[2 * q + 1]
                if half == 1:
                    dr = c * pr + s * qi
                    di = c * pi - s * qr
                else:
                    dr = c * pr - s * qi
                    di = c * pi + s * qr
                re, im = (dr, di) if re is None else (re + dr, im + di)
            level6[o6, 0, :, cols] = re
            level6[o6, 1, :, cols] = im

    for part in range(2):
        for r in range(0, rows6, 16):
            x = [level6[o, part, r : r + 16, :] for o in range(8)]
            for t in range(2):
                z = [x[k + 4] + x[k] if t == 0 else x[k + 4] - x[k] for k in range(4)]
                for q, (a, b) in enumerate(PAIRS):
                    mixed[2 * q, t, part, r : r + 16, :] = (z[a] + z[b]).astype(BF16)
                    mixed[2 * q + 1, t, part, r : r + 16, :] = (z[a] - z[b]).astype(BF16)

    for x in range(4):
        for part in range(2):
            rhs = jnp.concatenate([mixed[x, 0, part], mixed[x, 1, 1 - part]], axis=0)
            half6[x, part] = dot(m6[part], rhs).astype(BF16)

    block = 64
    quarter = cols5 // 4
    low_lane = lax.broadcasted_iota(jnp.int32, (block, quarter), 1) < quarter // 2
    for u in range(0, rows5, block):
        lhs = jnp.concatenate(
            [half6[x, part, u : u + block, :] for x in range(4) for part in range(2)], axis=0
        )
        y = dot(lhs, b6[...])
        for tile in range(4):
            cols = slice(tile * quarter, (tile + 1) * quarter)
            re = None
            for q in range(2):
                at = q * 4 * block
                pr = y[at : at + block, cols]
                pi = y[at + block : at + 2 * block, cols]
                qr = y[at + 2 * block : at + 3 * block, cols]
                qi = y[at + 3 * block : at + 4 * block, cols]
                place = (tile + q) % 4
                c = tab5[place % 2, 0, u : u + block, :]
                s = tab5[place % 2, 1, u : u + block, :]
                if place >= 2:
                    dr = c * pr + s * qi
                    di = c * pi - s * qr
                else:
                    dr = c * pr - s * qi
                    di = c * pi + s * qr
                if q == 0:
                    re, im = dr, di
                else:
                    re, im = re + dr, im + di
            if_low = jnp.where(low_lane, re, pltpu.roll(im, quarter // 2, 1)).astype(BF16)
            if_high = jnp.where(low_lane, pltpu.roll(re, quarter // 2, 1), im).astype(BF16)
            for r in range(0, block, 16):
                band = (u + r) // 16
                out[2 * tile * 16 + band, 0] = if_low[r : r + 16, :]
                out[(2 * tile + 1) * 16 + band, 0] = if_high[r : r + 16, :]


def aggregate(patterns7, polar_up7, azimuth_up7, polar_up6, azimuth_up6):
    children, _, rows7, cols7 = patterns7.shape
    rows6, rows5 = polar_up7.shape[0], polar_up6.shape[0]
    cols6, cols5 = azimuth_up7.shape[1], azimuth_up6.shape[1]
    clusters = children // 64
    pat = patterns7.reshape(children * 2 * rows7, cols7)
    top7, bottom7 = fold_factors(rows6, rows7)
    z = theta_phase(rows5)[:, None]
    cz = np.broadcast_to(np.cos(z), (rows5, rows6)).astype(np.float32)
    sz = np.broadcast_to(np.sin(z), (rows5, rows6)).astype(np.float32)
    f0, f1 = plane_phases(rows6, cols6, cols6 // 2)
    tab6 = np.stack([np.cos(f0), np.sin(f0), np.cos(f1), np.sin(f1)]).astype(np.float32)
    g0, _ = plane_phases(rows5, cols5, cols5 // 2)
    g0 = g0.reshape(rows5, 2, cols5 // 4).transpose(1, 0, 2)
    tab5 = np.stack([np.cos(g0), np.sin(g0)], axis=1).astype(np.float32)
    full = lambda shape: pl.BlockSpec(shape, lambda g: (0,) * len(shape))
    consts = (top7, bottom7, cz, sz, tab6, tab5)
    weights = (polar_up7, azimuth_up7, polar_up6, azimuth_up6)
    lines = pat.shape[0] // clusters
    return pl.pallas_call(
        aggregate_body,
        grid=(clusters,),
        in_specs=[pl.BlockSpec((lines, cols7), lambda g: (g, 0))]
        + [full(a.shape) for a in weights]
        + [full(a.shape) for a in consts],
        out_specs=pl.BlockSpec((128, 1, 16, 128), lambda g: (0, g, 0, 0)),
        out_shape=jax.ShapeDtypeStruct((128, clusters, 16, 128), BF16),
        scratch_shapes=[
            pltpu.VMEM((2 * rows6, 4 * rows7), BF16),
            pltpu.VMEM((2, rows5, 2 * rows6), BF16),
            pltpu.VMEM((8, 2, rows6, cols6), F32),
            pltpu.VMEM((4, 2, 2, rows6, cols6), BF16),
            pltpu.VMEM((4, 2, rows5, cols6), BF16),
        ],
        compiler_params=pltpu.CompilerParams(vmem_limit_bytes=VMEM_LIMIT),
        name="aggregate",
    )(pat, *weights, *[jnp.asarray(a) for a in consts])


def table_body(tr, out, spread):
    theta = pl.program_id(0)
    entries = out.shape[0]
    count = tr.shape[3]
    re = tr[0, 0]
    im = tr[1, 0]
    stack = jnp.concatenate([re, re, im, -im], axis=0)
    row = lax.broadcasted_iota(jnp.int32, (entries, count), 0)
    col = lax.broadcasted_iota(jnp.int32, (entries, count), 1)
    unit = jnp.where(row == col, 1.0, 0.0).astype(BF16)
    turned = dot_t(unit, stack)
    for j in range(2):
        spread[j, pl.ds(theta, entries, 16), :] = turned[:, j * 128 : (j + 1) * 128]

    @pl.when(theta == 15)
    def _():
        for j in range(2):
            out[:, j] = spread[j].reshape(entries, 16, 128).astype(BF16)


def transfer_table(transfer):
    count, _, rows, cols = transfer.shape
    entries = (count + 1 + 7) // 8 * 8
    return pl.pallas_call(
        table_body,
        grid=(rows,),
        in_specs=[pl.BlockSpec((2, 1, cols, count), lambda i: (0, i, 0, 0))],
        out_specs=pl.BlockSpec((entries, 2, rows, 2 * cols), lambda i: (0, 0, 0, 0)),
        out_shape=jax.ShapeDtypeStruct((entries, 2, rows, 2 * cols), BF16),
        scratch_shapes=[pltpu.VMEM((2, entries * rows, 2 * cols), F32)],
        compiler_params=pltpu.CompilerParams(vmem_limit_bytes=VMEM_LIMIT),
        name="transfer_table",
    )(transfer.transpose(1, 2, 3, 0))


def tree(terms):
    while len(terms) > 1:
        terms = [terms[i] + terms[i + 1] for i in range(0, len(terms), 2)]
    return terms[0]


def translate5_body(src, off, level, table, out, total):
    targets, rows, lanes = level.shape
    slots = src.shape[0]

    def one(t, carry):
        acc1 = jnp.zeros((rows, lanes), F32)
        acc2 = jnp.zeros((rows, lanes), F32)
        for j in range(0, slots, 4):
            first, second = [], []
            for i in range(4):
                x = level[src[j + i, t]]
                w = table.at[off[j + i, t]]
                first.append(w[0] * x)
                second.append(w[1] * x)
            acc1 = acc1 + tree(first).astype(F32)
            acc2 = acc2 + tree(second).astype(F32)
        total[pl.ds(pl.multiple_of(t * rows, rows), rows), :] = acc1 + pltpu.roll(acc2, lanes // 2, 1)
        return carry

    lax.fori_loop(0, targets, one, 0, unroll=2)
    unit = jnp.where(
        lax.broadcasted_iota(jnp.int32, (lanes, lanes), 0)
        == lax.broadcasted_iota(jnp.int32, (lanes, lanes), 1),
        1.0,
        0.0,
    ).astype(BF16)
    for theta in range(rows):
        turned = dot_t(unit, total[pl.ds(theta, targets, rows), :].astype(BF16)).astype(BF16)
        out[0, theta] = turned[: lanes // 2]
        out[1, theta] = turned[lanes // 2 :]


def translate5(level, table, sources, offsets):
    targets, rows, lanes = level.shape
    smem = pl.BlockSpec(memory_space=pltpu.SMEM)
    vmem = pl.BlockSpec(memory_space=pltpu.VMEM)
    turned = pl.pallas_call(
        translate5_body,
        in_specs=[smem, smem, vmem, vmem],
        out_specs=vmem,
        out_shape=jax.ShapeDtypeStruct((2, rows, lanes // 2, targets), BF16),
        scratch_shapes=[pltpu.VMEM((targets * rows, lanes), F32)],
        compiler_params=pltpu.CompilerParams(vmem_limit_bytes=VMEM_LIMIT),
        name="translate5",
    )(sources, offsets, level, table)
    return turned.transpose(3, 0, 1, 2)


def edge_picks():
    pick = np.zeros((96, 256), np.float32)
    for side in range(2):
        for n in range(48):
            parent, child, j = n // 24, n % 24 // 3, n % 3
            pick[side * 48 + n, parent * 128 + child * 16 + (13 if side == 0 else 0) + j] = 1.0
    return pick


def edges_body(level, pick, right, left, last, first, last_r, first_r, last_l, first_l):
    lane = lax.broadcasted_iota(jnp.int32, (1024, 256), 0)
    col = lax.broadcasted_iota(jnp.int32, (1024, 256), 1)
    side = col >> 7
    place = lane >> 7
    part = (lane >> 6) & 1
    j = col & 3
    hit = (
        (((col & 127) >> 4) == place)
        & (((col >> 3) & 1) == side)
        & (((col >> 2) & 1) == part)
        & (j < 3)
        & ((lane & 63) == jnp.where(side == 0, 61 + j, j))
    )
    spread = jnp.where(hit, 1.0, 0.0).astype(BF16)
    for g in range(8):
        lhs = jnp.concatenate([level[8 * g + i] for i in range(8)], axis=1)
        both = dot(lhs, spread).astype(BF16)
        right[g] = both[:, :128]
        left[g] = both[:, 128:]

    def rows_of(source, count, low, high):
        for i in range(count):
            rhs = jnp.concatenate([source[2 * i], source[2 * i + 1]], axis=0)
            both = dot(pick[...], rhs).astype(BF16)
            low[i] = both[:48]
            high[i] = both[48:]

    rows_of(level, 32, last, first)
    rows_of(right, 4, last_r, first_r)
    rows_of(left, 4, last_l, first_l)


def edges(level):
    shape = lambda *s: jax.ShapeDtypeStruct(s, BF16)
    pick = jnp.asarray(edge_picks(), BF16)
    return pl.pallas_call(
        edges_body,
        out_shape=(shape(8, 128, 128),) * 2 + (shape(32, 48, 128),) * 2 + (shape(4, 48, 128),) * 4,
        compiler_params=pltpu.CompilerParams(vmem_limit_bytes=VMEM_LIMIT),
        name="edges",
    )(level, pick)


def stencil_maps():
    ext = np.zeros((1, 224), np.int32)
    factor = np.zeros((2, 8, 224), np.float32)
    sign = np.zeros((4, 8))
    for q, (a, b) in enumerate(PAIRS):
        for h in range(2):
            sign[2 * q, a + 4 * h] = sign[2 * q, b + 4 * h] = 1.0
            sign[2 * q + 1, a + 4 * h] = 1.0
            sign[2 * q + 1, b + 4 * h] = -1.0
    for col in range(224):
        if col < 128:
            owner, child, ext[0, col] = (0, 1), col // 16, col % 16 + 3
        else:
            n = (col - 128) % 48
            owner, child = (n // 24,), n % 24 // 3
            ext[0, col] = n % 3 + (0 if col < 176 else 19)
        for parity in owner:
            for x in range(4):
                factor[parity, 2 * x, col] = sign[x, child]
                factor[parity, 2 * x + 1, col] = sign[x, child] * (1.0 if child >= 4 else -1.0)
    return ext, factor


def stencils_body(tap_u, weight_u, trig, tap_v, weight_v, ext, factor, polar, azimuth):
    rows = tap_u.shape[0]
    base = jnp.zeros((rows, ext.shape[1]), F32)
    for k in range(4):
        base = base + jnp.where(tap_u[:, k : k + 1] == ext[...], weight_u[:, k : k + 1], 0.0)
    for parity in range(2):
        for kind in range(8):
            turned = base * trig[:, kind % 2 : kind % 2 + 1]
            polar[parity, kind * rows : (kind + 1) * rows, :] = (
                turned * factor[parity, kind : kind + 1, :]
            ).astype(BF16)
    i = lax.broadcasted_iota(jnp.int32, (128, 128), 0)

    def fill(at, matrix, part, index):
        first = part == 0
        azimuth[index, at : at + 128, :128] = jnp.where(first, matrix, 0.0).astype(BF16)
        azimuth[index, at : at + 128, 128:] = jnp.where(first, 0.0, matrix).astype(BF16)
        azimuth[index, at + 128 : at + 256, :128] = jnp.where(first, 0.0, -matrix).astype(BF16)
        azimuth[index, at + 128 : at + 256, 128:] = jnp.where(first, matrix, 0.0).astype(BF16)

    def matrix_at(q):
        total = jnp.zeros((128, 128), F32)
        for k in range(4):
            total = total + jnp.where(tap_v[k : k + 1, :] == q, weight_v[k : k + 1, :], 0.0)
        return total

    own = matrix_at((i & 63) + 3)
    j = i & 3
    halo = jnp.where(j < 3, matrix_at(j + 67 * ((i >> 3) & 1)), 0.0)
    for index in range(8):
        fill(0, own, i >> 6, index)
        fill(256, jnp.where((i >> 4) == index, halo, 0.0), (i >> 2) & 1, index)


def stencils(tap_u, weight_u, trig, tap_v, weight_v):
    ext, factor = stencil_maps()
    rows = tap_u.shape[0]
    return pl.pallas_call(
        stencils_body,
        out_shape=(
            jax.ShapeDtypeStruct((2, 8 * rows, 224), BF16),
            jax.ShapeDtypeStruct((8, 512, 256), BF16),
        ),
        compiler_params=pltpu.CompilerParams(vmem_limit_bytes=VMEM_LIMIT),
        name="stencils",
    )(tap_u, weight_u, trig, tap_v, weight_v, jnp.asarray(ext), jnp.asarray(factor))


def top_body(
    src, off, level, from_left, from_right, low, high, low_l, low_r, high_l, high_r, polar, azimuth,
    tab, transfer, out, table, half, level4, sem,
):
    count = transfer.shape[0]
    fetch = pltpu.make_async_copy(transfer, table.at[pl.ds(0, count)], sem)
    fetch.start()
    table[count] = jnp.zeros(table.shape[1:], BF16)

    def theta_stage(i, carry):
        for parity in range(2):
            rhs = jnp.concatenate([level[2 * i + parity], low[i], high[i]], axis=0)
            half[2 * i + parity] = dot(polar[parity], rhs).astype(BF16)
        return carry

    lax.fori_loop(0, 32, theta_stage, 0, unroll=4)
    for i in range(4):
        rows_low = low_l[i] + low_r[i]
        rows_high = high_l[i] + high_r[i]
        for parity in range(2):
            g = 2 * i + parity
            rhs = jnp.concatenate([from_left[g] + from_right[g], rows_low, rows_high], axis=0)
            half[64 + g] = dot(polar[parity], rhs).astype(BF16)

    def phi_stage(place, carry):
        rows = []
        for g in range(8):
            for x in range(4):
                a = slice(64 * x, 64 * x + 32)
                b = slice(64 * x + 32, 64 * x + 64)
                p = 8 * g + place
                rows.append(
                    jnp.concatenate([half[p, a], half[p, b], half[64 + g, a], half[64 + g, b]], axis=1)
                )
        y = dot(jnp.concatenate(rows, axis=0), azimuth[place])
        for g in range(8):
            re = im = None
            for q in range(2):
                at = 128 * g + 64 * q
                pr = y[at : at + 32, :128]
                pi = y[at : at + 32, 128:]
                qr = y[at + 32 : at + 64, :128]
                qi = y[at + 32 : at + 64, 128:]
                c = tab[2 * q]
                s = tab[2 * q + 1]
                dr = c * pr - s * qi
                di = c * pi + s * qr
                re, im = (dr, di) if q == 0 else (re + dr, im + di)
            level4[8 * g + place, 0] = re.astype(BF16)
            level4[8 * g + place, 1] = im.astype(BF16)
        return carry

    lax.fori_loop(0, 8, phi_stage, 0)
    fetch.wait()
    slots = src.shape[0]

    def one(t, carry):
        re = jnp.zeros((32, 128), F32)
        im = jnp.zeros((32, 128), F32)
        for j in range(0, slots, 2):
            terms_r, terms_i = [], []
            for i in range(2):
                x = level4.at[src[j + i, t]]
                w = table.at[off[j + i, t]]
                xr, xi = x[0], x[1]
                wr, wi = w[0], w[1]
                terms_r.append(wr * xr - wi * xi)
                terms_i.append(wr * xi + wi * xr)
            re = re + tree(terms_r).astype(F32)
            im = im + tree(terms_i).astype(F32)
        out[t, 0] = re.astype(BF16)
        out[t, 1] = im.astype(BF16)
        return carry

    lax.fori_loop(0, out.shape[0], one, 0)


def top_level(level, halos, polar, azimuth, tab, transfer, sources, offsets):
    count, _, rows, cols = transfer.shape
    smem = pl.BlockSpec(memory_space=pltpu.SMEM)
    vmem = pl.BlockSpec(memory_space=pltpu.VMEM)
    parents = level.shape[0]
    return pl.pallas_call(
        top_body,
        in_specs=[smem, smem] + [vmem] * 12 + [pl.BlockSpec(memory_space=pl.ANY)],
        out_specs=vmem,
        out_shape=jax.ShapeDtypeStruct((parents, 2, rows, cols), BF16),
        scratch_shapes=[
            pltpu.VMEM((count + 1, 2, rows, cols), BF16),
            pltpu.VMEM((72, 256, 128), BF16),
            pltpu.VMEM((parents, 2, rows, cols), BF16),
            pltpu.SemaphoreType.DMA,
        ],
        compiler_params=pltpu.CompilerParams(vmem_limit_bytes=VMEM_LIMIT),
        name="top_level",
    )(sources, offsets, level, *halos, polar, azimuth, tab, transfer)


def shards(
    patterns7,
    polar_up7,
    azimuth_up7,
    polar_up6,
    azimuth_up6,
    polar_first,
    polar_weights,
    azimuth_first,
    azimuth_weights,
    transfer5,
    sources5,
    offsets5,
    transfer4,
    sources4,
    offsets4,
):
    bands = lax.axis_size("ang")
    blocks = lax.axis_size("clu")
    band = lax.axis_index("ang")
    block = lax.axis_index("clu")

    send = aggregate(patterns7, polar_up7, azimuth_up7, polar_up6, azimuth_up6)
    arrived = lax.all_to_all(send, ("clu", "ang"), split_axis=0, concat_axis=0, tiled=True)

    count5 = transfer5.shape[0]
    count4 = transfer4.shape[0]
    table5 = transfer_table(transfer5)
    src5 = jnp.maximum(sources5.T, 0)
    off5 = jnp.where(offsets5.T < 0, count5, offsets5.T)
    src4 = jnp.maximum(sources4.T, 0)
    off4 = jnp.where(offsets4.T < 0, count4, offsets4.T)
    rows4 = polar_first.shape[0]
    cols4 = azimuth_first.shape[0]
    band_rows = rows4 // bands
    block_cols = cols4 // blocks
    taps = jnp.arange(4, dtype=jnp.int32)
    tap_u = lax.dynamic_slice_in_dim(polar_first, band * band_rows, band_rows, 0)
    tap_u = (tap_u - band * (band_rows // 2) + 3)[:, None] + taps[None, :]
    weight_u = lax.dynamic_slice_in_dim(polar_weights, band * band_rows, band_rows, 0).astype(F32)
    tap_v = lax.dynamic_slice_in_dim(azimuth_first, block * block_cols, block_cols, 0)
    tap_v = (tap_v[None, :] + taps[:, None] - block * (block_cols // 2) + 3) % (cols4 // 2)
    weight_v = lax.dynamic_slice_in_dim(azimuth_weights, block * block_cols, block_cols, 0)
    weight_v = weight_v.T.astype(F32)
    theta = (jnp.arange(band_rows, dtype=jnp.int32) + band * band_rows).astype(F32)
    theta = (theta + 0.5) * (math.pi / rows4)
    phi = (jnp.arange(block_cols, dtype=jnp.int32) + block * block_cols).astype(F32)
    phi = phi * (2.0 * math.pi / cols4)
    scale = rows4 / 8.0
    lift = scale * jnp.cos(theta)
    trig = jnp.stack([jnp.cos(lift), jnp.sin(lift)], axis=1)
    x = jnp.sin(theta)[:, None] * jnp.cos(phi)[None, :]
    y = jnp.sin(theta)[:, None] * jnp.sin(phi)[None, :]
    f0 = scale * (x + y)
    f1 = scale * (x - y)
    tab = jnp.stack([jnp.cos(f0), jnp.sin(f0), jnp.cos(f1), jnp.sin(f1)])
    polar, azimuth = stencils(tap_u, weight_u, trig, tap_v, weight_v)

    level = arrived.reshape(64, 128, 128)
    right, left, last, first, last_r, first_r, last_l, first_l = edges(level)

    def moved(value, step_block, step_band):
        pairs = []
        for c in range(blocks):
            for a in range(bands):
                to = a + step_band
                if 0 <= to < bands:
                    pairs.append((c * bands + a, (c + step_block) % blocks * bands + to))
        return lax.ppermute(value, ("clu", "ang"), pairs)

    halos = (
        moved(right, 1, 0),
        moved(left, -1, 0),
        moved(last, 0, 1),
        moved(first, 0, -1),
        moved(last_r, 1, 1),
        moved(last_l, -1, 1),
        moved(first_r, 1, -1),
        moved(first_l, -1, -1),
    )
    translated5 = translate5(arrived.reshape(512, 16, 128), table5, src5, off5)
    translated4 = top_level(level, halos, polar, azimuth, tab, transfer4, src4, off4)
    return (translated5, translated4)


def solution(mesh):
    in_specs = (
        P(("clu", "ang"), None, None, None),
        P(),
        P(),
        P(),
        P(),
        P(),
        P(),
        P(),
        P(),
        P(None, None, "ang", "clu"),
        P(),
        P(),
        P(None, None, "ang", "clu"),
        P(),
        P(),
    )
    out_specs = (P(None, None, "ang", "clu"), P(None, None, "ang", "clu"))
    return jax.shard_map(shards, mesh=mesh, in_specs=in_specs, out_specs=out_specs, check_vma=False)
```

```python
import math

import jax
import jax.numpy as jnp
import numpy as np
from jax import lax
from jax.experimental import pallas as pl
from jax.experimental.pallas import tpu as pltpu
from jax.sharding import PartitionSpec as P

F32 = jnp.float32
BF16 = jnp.bfloat16


PAIRS = ((3, 0), (1, 2))


def theta_phase(rows):
    return rows / 8.0 * np.cos(np.pi * (np.arange(rows) + 0.5) / rows)


def plane_phases(rows, cols, count):
    theta = np.pi * (np.arange(rows) + 0.5) / rows
    phi = 2.0 * np.pi * np.arange(count) / cols
    x = np.sin(theta)[:, None] * np.cos(phi)[None, :]
    y = np.sin(theta)[:, None] * np.sin(phi)[None, :]
    return rows / 8.0 * (x + y), rows / 8.0 * (x - y)


def fold_factors(rows, inner):
    phase = theta_phase(rows)[:, None]
    cosine = np.broadcast_to(np.cos(phase), (rows, inner))
    sine = np.broadcast_to(np.sin(phase), (rows, inner))
    top = np.concatenate([cosine, sine, cosine, -sine], axis=1)
    bottom = np.concatenate([-sine, cosine, sine, cosine], axis=1)
    return top.astype(np.float32), bottom.astype(np.float32)


def dot(a, b):
    return jnp.dot(a, b, preferred_element_type=F32)


def dot_t(a, b):
    return lax.dot_general(a, b, (((1,), (1,)), ((), ())), preferred_element_type=F32)


def aggregate_body(
    pat, a7, b7, a6, b6, top7, bottom7, cz, sz, tab6, tab5, out, m7, m6, level6, mixed, half6
):
    rows7, rows6, rows5 = a7.shape[1], a7.shape[0], a6.shape[0]
    cols6, cols5 = b7.shape[1], b6.shape[1]

    @pl.when(pl.program_id(0) == 0)
    def _():
        src = lax.broadcasted_iota(jnp.int32, (rows7, 4 * rows7), 0)
        dst = lax.broadcasted_iota(jnp.int32, (rows7, 4 * rows7), 1)
        spread = jnp.where((dst & (rows7 - 1)) == src, 1.0, 0.0).astype(BF16)
        wide = dot(a7[...], spread)
        m7[0:rows6, :] = (wide * top7[...]).astype(BF16)
        m7[rows6 : 2 * rows6, :] = (wide * bottom7[...]).astype(BF16)
        base = a6[...].astype(F32)
        c = base * cz[...]
        s = base * sz[...]
        m6[0, :, 0:rows6] = c.astype(BF16)
        m6[0, :, rows6 : 2 * rows6] = (-s).astype(BF16)
        m6[1, :, 0:rows6] = c.astype(BF16)
        m6[1, :, rows6 : 2 * rows6] = s.astype(BF16)

    step = 2 * rows7
    for o6 in range(8):
        base = o6 * 8 * step
        parts = []
        for k in range(4):
            low = pat[base + k * step : base + (k + 1) * step, :]
            high = pat[base + (k + 4) * step : base + (k + 5) * step, :]
            parts.append(jnp.concatenate([low, high], axis=0))
        lanes = parts[0].shape[1]
        h = dot(m7[...], jnp.concatenate(parts, axis=1))
        rows = []
        for a, b in PAIRS:
            ya = h[:, a * lanes : (a + 1) * lanes]
            yb = h[:, b * lanes : (b + 1) * lanes]
            rows.append((ya + yb).astype(BF16))
            rows.append((ya - yb).astype(BF16))
        y = dot(jnp.concatenate(rows, axis=0), b7[...])
        for half in range(2):
            cols = slice(half * (cols6 // 2), (half + 1) * (cols6 // 2))
            re = None
            for q in range(2):
                at = q * 4 * rows6
                pr = y[at : at + rows6, cols]
                pi = y[at + rows6 : at + 2 * rows6, cols]
                qr = y[at + 2 * rows6 : at + 3 * rows6, cols]
                qi = y[at + 3 * rows6 : at + 4 * rows6, cols]
                c = tab6[2 * q]
                s = tab6[2 * q + 1]
                if half == 1:
                    dr = c * pr + s * qi
                    di = c * pi - s * qr
                else:
                    dr = c * pr - s * qi
                    di = c * pi + s * qr
                re, im = (dr, di) if re is None else (re + dr, im + di)
            level6[o6, 0, :, cols] = re
            level6[o6, 1, :, cols] = im

    for part in range(2):
        for r in range(0, rows6, 16):
            x = [level6[o, part, r : r + 16, :] for o in range(8)]
            for t in range(2):
                z = [x[k + 4] + x[k] if t == 0 else x[k + 4] - x[k] for k in range(4)]
                for q, (a, b) in enumerate(PAIRS):
                    mixed[2 * q, t, part, r : r + 16, :] = (z[a] + z[b]).astype(BF16)
                    mixed[2 * q + 1, t, part, r : r + 16, :] = (z[a] - z[b]).astype(BF16)

    for x in range(4):
        for part in range(2):
            rhs = jnp.concatenate([mixed[x, 0, part], mixed[x, 1, 1 - part]], axis=0)
            half6[x, part] = dot(m6[part], rhs).astype(BF16)

    block = 64
    quarter = cols5 // 4
    low_lane = lax.broadcasted_iota(jnp.int32, (block, quarter), 1) < quarter // 2
    for u in range(0, rows5, block):
        lhs = jnp.concatenate(
            [half6[x, part, u : u + block, :] for x in range(4) for part in range(2)], axis=0
        )
        y = dot(lhs, b6[...])
        for tile in range(4):
            cols = slice(tile * quarter, (tile + 1) * quarter)
            re = None
            for q in range(2):
                at = q * 4 * block
                pr = y[at : at + block, cols]
                pi = y[at + block : at + 2 * block, cols]
                qr = y[at + 2 * block : at + 3 * block, cols]
                qi = y[at + 3 * block : at + 4 * block, cols]
                place = (tile + q) % 4
                c = tab5[place % 2, 0, u : u + block, :]
                s = tab5[place % 2, 1, u : u + block, :]
                if place >= 2:
                    dr = c * pr + s * qi
                    di = c * pi - s * qr
                else:
                    dr = c * pr - s * qi
                    di = c * pi + s * qr
                if q == 0:
                    re, im = dr, di
                else:
                    re, im = re + dr, im + di
            if_low = jnp.where(low_lane, re, pltpu.roll(im, quarter // 2, 1)).astype(BF16)
            if_high = jnp.where(low_lane, pltpu.roll(re, quarter // 2, 1), im).astype(BF16)
            for r in range(0, block, 16):
                band = (u + r) // 16
                out[2 * tile * 16 + band, 0] = if_low[r : r + 16, :]
                out[(2 * tile + 1) * 16 + band, 0] = if_high[r : r + 16, :]


def aggregate(patterns7, polar_up7, azimuth_up7, polar_up6, azimuth_up6):
    children, _, rows7, cols7 = patterns7.shape
    rows6, rows5 = polar_up7.shape[0], polar_up6.shape[0]
    cols6, cols5 = azimuth_up7.shape[1], azimuth_up6.shape[1]
    clusters = children // 64
    pat = patterns7.reshape(children * 2 * rows7, cols7)
    top7, bottom7 = fold_factors(rows6, rows7)
    z = theta_phase(rows5)[:, None]
    cz = np.broadcast_to(np.cos(z), (rows5, rows6)).astype(np.float32)
    sz = np.broadcast_to(np.sin(z), (rows5, rows6)).astype(np.float32)
    f0, f1 = plane_phases(rows6, cols6, cols6 // 2)
    tab6 = np.stack([np.cos(f0), np.sin(f0), np.cos(f1), np.sin(f1)]).astype(np.float32)
    g0, _ = plane_phases(rows5, cols5, cols5 // 2)
    g0 = g0.reshape(rows5, 2, cols5 // 4).transpose(1, 0, 2)
    tab5 = np.stack([np.cos(g0), np.sin(g0)], axis=1).astype(np.float32)
    full = lambda shape: pl.BlockSpec(shape, lambda g: (0,) * len(shape))
    consts = (top7, bottom7, cz, sz, tab6, tab5)
    weights = (polar_up7, azimuth_up7, polar_up6, azimuth_up6)
    lines = pat.shape[0] // clusters
    return pl.pallas_call(
        aggregate_body,
        grid=(clusters,),
        in_specs=[pl.BlockSpec((lines, cols7), lambda g: (g, 0))]
        + [full(a.shape) for a in weights]
        + [full(a.shape) for a in consts],
        out_specs=pl.BlockSpec((128, 1, 16, 128), lambda g: (0, g, 0, 0)),
        out_shape=jax.ShapeDtypeStruct((128, clusters, 16, 128), BF16),
        scratch_shapes=[
            pltpu.VMEM((2 * rows6, 4 * rows7), BF16),
            pltpu.VMEM((2, rows5, 2 * rows6), BF16),
            pltpu.VMEM((8, 2, rows6, cols6), F32),
            pltpu.VMEM((4, 2, 2, rows6, cols6), BF16),
            pltpu.VMEM((4, 2, rows5, cols6), BF16),
        ],
        compiler_params=pltpu.CompilerParams(vmem_limit_bytes=58 * 1024 * 1024),
        name="aggregate",
    )(pat, *weights, *[jnp.asarray(a) for a in consts])


def table_body(tr, out):
    theta = pl.program_id(0)
    entries = out.shape[0] // 16
    count = tr.shape[4]
    stack = jnp.concatenate([tr[0, 0, 0], tr[0, 1, 0], tr[1, 0, 0], tr[1, 1, 0]], axis=0)
    row = lax.broadcasted_iota(jnp.int32, (entries, count), 0)
    col = lax.broadcasted_iota(jnp.int32, (entries, count), 1)
    unit = jnp.where(row == col, 1.0, 0.0).astype(BF16)
    turned = dot_t(unit, stack)
    out[pl.ds(theta, entries, 16), :] = turned[:, :128]
    out[pl.ds(theta + 8, entries, 16), :] = turned[:, 128:]


def transfer_table(transfer):
    count, _, rows, cols = transfer.shape
    entries = (count + 1 + 7) // 8 * 8
    turned = transfer.transpose(1, 2, 3, 0).reshape(2, 2, rows // 2, cols, count)
    return pl.pallas_call(
        table_body,
        grid=(rows // 2,),
        in_specs=[pl.BlockSpec((2, 2, 1, cols, count), lambda i: (0, 0, i, 0, 0))],
        out_specs=pl.BlockSpec((entries * 16, 128), lambda i: (0, 0)),
        out_shape=jax.ShapeDtypeStruct((entries * 16, 128), F32),
        compiler_params=pltpu.CompilerParams(vmem_limit_bytes=12 * 1024 * 1024),
        name="transfer_table",
    )(turned)


def tree(terms):
    while len(terms) > 1:
        terms = [terms[i] + terms[i + 1] for i in range(0, len(terms), 2)]
    return terms[0]


def translate5_body(src, off, level, table, out, tiles, total):
    targets, rows, lanes = level.shape
    slots = src.shape[0] // targets
    low = lax.broadcasted_iota(jnp.int32, (8, lanes), 1) < lanes // 2

    def widen(t, carry):
        x = level[t].astype(F32)
        upper, lower = x[:8], x[8:]
        at = pl.multiple_of(t * 16, 16)
        tiles[pl.ds(at, 8), :] = jnp.where(low, upper, pltpu.roll(lower, lanes // 2, 1))
        tiles[pl.ds(at + 8, 8), :] = jnp.where(low, pltpu.roll(upper, lanes // 2, 1), lower)
        return carry

    lax.fori_loop(0, targets, widen, 0, unroll=16)

    def one(t, carry):
        terms_r, terms_i = [], []
        for j in range(slots):
            s = pl.multiple_of(src[t * slots + j], 16)
            o = pl.multiple_of(off[t * slots + j], 16)
            xr = tiles[pl.ds(s, 8), :]
            xi = tiles[pl.ds(s + 8, 8), :]
            wr = table[pl.ds(o, 8), :]
            wi = table[pl.ds(o + 8, 8), :]
            terms_r.append(wr * xr - wi * xi)
            terms_i.append(wr * xi + wi * xr)
        at = pl.multiple_of(t * 16, 16)
        total[pl.ds(at, 8), :] = tree(terms_r)
        total[pl.ds(at + 8, 8), :] = tree(terms_i)
        return carry

    lax.fori_loop(0, targets, one, 0, unroll=2)
    unit = jnp.where(
        lax.broadcasted_iota(jnp.int32, (lanes, lanes), 0)
        == lax.broadcasted_iota(jnp.int32, (lanes, lanes), 1),
        1.0,
        0.0,
    ).astype(BF16)
    for row in range(16):
        turned = dot_t(unit, total[pl.ds(row, targets, 16), :].astype(BF16)).astype(BF16)
        out[row // 8, row % 8] = turned[: lanes // 2]
        out[row // 8, row % 8 + 8] = turned[lanes // 2 :]


def translate5(level, table, sources, offsets):
    targets, rows, lanes = level.shape
    smem = pl.BlockSpec(memory_space=pltpu.SMEM)
    vmem = pl.BlockSpec(memory_space=pltpu.VMEM)
    turned = pl.pallas_call(
        translate5_body,
        in_specs=[smem, smem, vmem, vmem],
        out_specs=vmem,
        out_shape=jax.ShapeDtypeStruct((2, rows, lanes // 2, targets), BF16),
        scratch_shapes=[
            pltpu.VMEM((targets * 16, lanes), F32),
            pltpu.VMEM((targets * 16, lanes), F32),
        ],
        compiler_params=pltpu.CompilerParams(vmem_limit_bytes=24 * 1024 * 1024),
        name="translate5",
    )(sources, offsets, level, table)
    return turned.transpose(3, 0, 1, 2)


def edge_picks():
    pick = np.zeros((96, 256), np.float32)
    for side in range(2):
        for n in range(48):
            parent, child, j = n // 24, n % 24 // 3, n % 3
            pick[side * 48 + n, parent * 128 + child * 16 + (13 if side == 0 else 0) + j] = 1.0
    return pick


def edges_body(level, pick, right, left, last, first):
    lane = lax.broadcasted_iota(jnp.int32, (1024, 256), 0)
    col = lax.broadcasted_iota(jnp.int32, (1024, 256), 1)
    side = col >> 7
    place = lane >> 7
    part = (lane >> 6) & 1
    j = col & 3
    hit = (
        (((col & 127) >> 4) == place)
        & (((col >> 3) & 1) == side)
        & (((col >> 2) & 1) == part)
        & (j < 3)
        & ((lane & 63) == jnp.where(side == 0, 61 + j, j))
    )
    spread = jnp.where(hit, 1.0, 0.0).astype(BF16)
    for g in range(8):
        lhs = jnp.concatenate([level[8 * g + i] for i in range(8)], axis=1)
        both = dot(lhs, spread).astype(BF16)
        right[g] = both[:, :128]
        left[g] = both[:, 128:]

    edge_rows(level, pick, last, first)


def edge_rows(source, pick, last, first):
    for i in range(last.shape[0]):
        rhs = jnp.concatenate([source[2 * i], source[2 * i + 1]], axis=0)
        both = dot(pick[...], rhs).astype(BF16)
        last[i] = both[:48]
        first[i] = both[48:]


def edges(level):
    shape = lambda *s: jax.ShapeDtypeStruct(s, BF16)
    pick = jnp.asarray(edge_picks(), BF16)
    return pl.pallas_call(
        edges_body,
        out_shape=(shape(8, 128, 128),) * 2 + (shape(32, 48, 128),) * 2,
        compiler_params=pltpu.CompilerParams(vmem_limit_bytes=10 * 1024 * 1024),
        name="edges",
    )(level, pick)


def corners_body(from_left, from_right, pick, sides, last, first):
    for g in range(sides.shape[0]):
        sides[g] = from_left[g] + from_right[g]
    edge_rows(sides, pick, last, first)


def corners(from_left, from_right):
    shape = lambda *s: jax.ShapeDtypeStruct(s, BF16)
    pick = jnp.asarray(edge_picks(), BF16)
    return pl.pallas_call(
        corners_body,
        out_shape=(shape(8, 128, 128),) + (shape(4, 48, 128),) * 2,
        compiler_params=pltpu.CompilerParams(vmem_limit_bytes=4 * 1024 * 1024),
        name="corners",
    )(from_left, from_right, pick)


def stencil_maps():
    ext = np.zeros((1, 224), np.int32)
    factor = np.zeros((2, 8, 224), np.float32)
    sign = np.zeros((4, 8))
    for q, (a, b) in enumerate(PAIRS):
        for h in range(2):
            sign[2 * q, a + 4 * h] = sign[2 * q, b + 4 * h] = 1.0
            sign[2 * q + 1, a + 4 * h] = 1.0
            sign[2 * q + 1, b + 4 * h] = -1.0
    for col in range(224):
        if col < 128:
            owner, child, ext[0, col] = (0, 1), col // 16, col % 16 + 3
        else:
            n = (col - 128) % 48
            owner, child = (n // 24,), n % 24 // 3
            ext[0, col] = n % 3 + (0 if col < 176 else 19)
        for parity in owner:
            for x in range(4):
                factor[parity, 2 * x, col] = sign[x, child]
                factor[parity, 2 * x + 1, col] = sign[x, child] * (1.0 if child >= 4 else -1.0)
    return ext, factor


def stencils_body(tap_u, weight_u, trig, tap_v, weight_v, ext, factor, polar, azimuth):
    rows = tap_u.shape[0]
    base = jnp.zeros((rows, ext.shape[1]), F32)
    for k in range(4):
        base = base + jnp.where(tap_u[:, k : k + 1] == ext[...], weight_u[:, k : k + 1], 0.0)
    for parity in range(2):
        for kind in range(8):
            turned = base * trig[:, kind % 2 : kind % 2 + 1]
            polar[parity, kind * rows : (kind + 1) * rows, :] = (
                turned * factor[parity, kind : kind + 1, :]
            ).astype(BF16)
    i = lax.broadcasted_iota(jnp.int32, (128, 128), 0)

    def fill(at, matrix, part, index):
        first = part == 0
        azimuth[index, at : at + 128, :128] = jnp.where(first, matrix, 0.0).astype(BF16)
        azimuth[index, at : at + 128, 128:] = jnp.where(first, 0.0, matrix).astype(BF16)
        azimuth[index, at + 128 : at + 256, :128] = jnp.where(first, 0.0, -matrix).astype(BF16)
        azimuth[index, at + 128 : at + 256, 128:] = jnp.where(first, matrix, 0.0).astype(BF16)

    def matrix_at(q):
        total = jnp.zeros((128, 128), F32)
        for k in range(4):
            total = total + jnp.where(tap_v[k : k + 1, :] == q, weight_v[k : k + 1, :], 0.0)
        return total

    own = matrix_at((i & 63) + 3)
    j = i & 3
    halo = jnp.where(j < 3, matrix_at(j + 67 * ((i >> 3) & 1)), 0.0)
    for index in range(8):
        fill(0, own, i >> 6, index)
        fill(256, jnp.where((i >> 4) == index, halo, 0.0), (i >> 2) & 1, index)


def stencils(tap_u, weight_u, trig, tap_v, weight_v):
    ext, factor = stencil_maps()
    rows = tap_u.shape[0]
    return pl.pallas_call(
        stencils_body,
        out_shape=(
            jax.ShapeDtypeStruct((2, 8 * rows, 224), BF16),
            jax.ShapeDtypeStruct((8, 512, 256), BF16),
        ),
        compiler_params=pltpu.CompilerParams(vmem_limit_bytes=8 * 1024 * 1024),
        name="stencils",
    )(tap_u, weight_u, trig, tap_v, weight_v, jnp.asarray(ext), jnp.asarray(factor))


def theta_stage(level, low, high, polar, half):
    for i in range(low.shape[0]):
        for parity in range(2):
            rhs = jnp.concatenate([level[2 * i + parity], low[i], high[i]], axis=0)
            half[2 * i + parity] = dot(polar[parity], rhs).astype(BF16)


def theta_level(level, low, high, polar):
    parents = level.shape[0]
    return pl.pallas_call(
        theta_stage,
        out_shape=jax.ShapeDtypeStruct((parents, polar.shape[1], level.shape[2]), BF16),
        compiler_params=pltpu.CompilerParams(vmem_limit_bytes=14 * 1024 * 1024),
        name="theta_level",
    )(level, low, high, polar)


def top_body(
    src, off, half, sides, low, high, polar, azimuth, tab, transfer, out, table, side_half, level4, sem
):
    count = transfer.shape[0]
    fetch = pltpu.make_async_copy(transfer, table.at[pl.ds(0, count)], sem)
    fetch.start()
    table[count] = jnp.zeros(table.shape[1:], BF16)
    theta_stage(sides, low, high, polar, side_half)

    def phi_stage(place, carry):
        rows = []
        for g in range(8):
            for x in range(4):
                a = slice(64 * x, 64 * x + 32)
                b = slice(64 * x + 32, 64 * x + 64)
                p = 8 * g + place
                rows.append(
                    jnp.concatenate([half[p, a], half[p, b], side_half[g, a], side_half[g, b]], axis=1)
                )
        y = dot(jnp.concatenate(rows, axis=0), azimuth[place])
        for g in range(8):
            re = im = None
            for q in range(2):
                at = 128 * g + 64 * q
                pr = y[at : at + 32, :128]
                pi = y[at : at + 32, 128:]
                qr = y[at + 32 : at + 64, :128]
                qi = y[at + 32 : at + 64, 128:]
                c = tab[2 * q]
                s = tab[2 * q + 1]
                dr = c * pr - s * qi
                di = c * pi + s * qr
                re, im = (dr, di) if q == 0 else (re + dr, im + di)
            at = pl.multiple_of((8 * g + place) * 64, 64)
            level4[pl.ds(at, 32), :] = re
            level4[pl.ds(at + 32, 32), :] = im
        return carry

    lax.fori_loop(0, 8, phi_stage, 0)
    fetch.wait()
    targets = out.shape[0]
    slots = src.shape[0] // targets

    def one(t, carry):
        re = [jnp.zeros((8, 128), F32)] * 4
        im = [jnp.zeros((8, 128), F32)] * 4
        for j in range(slots):
            at = pl.multiple_of(src[t * slots + j], 64)
            w = table.at[off[t * slots + j]]
            for r in range(4):
                xr = level4[pl.ds(at + 8 * r, 8), :]
                xi = level4[pl.ds(at + 32 + 8 * r, 8), :]
                wr = w[0, 8 * r : 8 * r + 8].astype(F32)
                wi = w[1, 8 * r : 8 * r + 8].astype(F32)
                re[r] = re[r] + (wr * xr - wi * xi)
                im[r] = im[r] + (wr * xi + wi * xr)
        for r in range(4):
            out[t, 0, 8 * r : 8 * r + 8] = re[r].astype(BF16)
            out[t, 1, 8 * r : 8 * r + 8] = im[r].astype(BF16)
        return carry

    lax.fori_loop(0, targets, one, 0)


def top_level(half, sides, low, high, polar, azimuth, tab, transfer, sources, offsets):
    count, _, rows, cols = transfer.shape
    smem = pl.BlockSpec(memory_space=pltpu.SMEM)
    vmem = pl.BlockSpec(memory_space=pltpu.VMEM)
    parents = half.shape[0]
    return pl.pallas_call(
        top_body,
        in_specs=[smem, smem] + [vmem] * 7 + [pl.BlockSpec(memory_space=pl.ANY)],
        out_specs=vmem,
        out_shape=jax.ShapeDtypeStruct((parents, 2, rows, cols), BF16),
        scratch_shapes=[
            pltpu.VMEM((count + 1, 2, rows, cols), BF16),
            pltpu.VMEM((sides.shape[0],) + half.shape[1:], BF16),
            pltpu.VMEM((parents * 2 * rows, cols), F32),
            pltpu.SemaphoreType.DMA,
        ],
        compiler_params=pltpu.CompilerParams(vmem_limit_bytes=24 * 1024 * 1024),
        name="top_level",
    )(sources, offsets, half, sides, low, high, polar, azimuth, tab, transfer)


def flat_lists(sources, offsets, dead, source_rows, factor_rows):
    src = jnp.maximum(sources, 0) * source_rows
    off = jnp.where(offsets < 0, dead, offsets) * factor_rows
    return src.reshape(-1), off.reshape(-1)


def shards(
    patterns7,
    polar_up7,
    azimuth_up7,
    polar_up6,
    azimuth_up6,
    polar_first,
    polar_weights,
    azimuth_first,
    azimuth_weights,
    transfer5,
    sources5,
    offsets5,
    transfer4,
    sources4,
    offsets4,
):
    bands = lax.axis_size("ang")
    blocks = lax.axis_size("clu")
    band = lax.axis_index("ang")
    block = lax.axis_index("clu")

    send = aggregate(patterns7, polar_up7, azimuth_up7, polar_up6, azimuth_up6)
    arrived = lax.all_to_all(send, ("clu", "ang"), split_axis=0, concat_axis=0, tiled=True)

    count5 = transfer5.shape[0]
    count4 = transfer4.shape[0]
    table5 = transfer_table(transfer5)
    src5, off5 = flat_lists(sources5, offsets5, count5, 16, 16)
    src4, off4 = flat_lists(sources4, offsets4, count4, 64, 1)
    rows4 = polar_first.shape[0]
    cols4 = azimuth_first.shape[0]
    band_rows = rows4 // bands
    block_cols = cols4 // blocks
    taps = jnp.arange(4, dtype=jnp.int32)
    tap_u = lax.dynamic_slice_in_dim(polar_first, band * band_rows, band_rows, 0)
    tap_u = (tap_u - band * (band_rows // 2) + 3)[:, None] + taps[None, :]
    weight_u = lax.dynamic_slice_in_dim(polar_weights, band * band_rows, band_rows, 0).astype(F32)
    tap_v = lax.dynamic_slice_in_dim(azimuth_first, block * block_cols, block_cols, 0)
    tap_v = (tap_v[None, :] + taps[:, None] - block * (block_cols // 2) + 3) % (cols4 // 2)
    weight_v = lax.dynamic_slice_in_dim(azimuth_weights, block * block_cols, block_cols, 0)
    weight_v = weight_v.T.astype(F32)
    theta = (jnp.arange(band_rows, dtype=jnp.int32) + band * band_rows).astype(F32)
    theta = (theta + 0.5) * (math.pi / rows4)
    phi = (jnp.arange(block_cols, dtype=jnp.int32) + block * block_cols).astype(F32)
    phi = phi * (2.0 * math.pi / cols4)
    scale = rows4 / 8.0
    lift = scale * jnp.cos(theta)
    trig = jnp.stack([jnp.cos(lift), jnp.sin(lift)], axis=1)
    x = jnp.sin(theta)[:, None] * jnp.cos(phi)[None, :]
    y = jnp.sin(theta)[:, None] * jnp.sin(phi)[None, :]
    f0 = scale * (x + y)
    f1 = scale * (x - y)
    tab = jnp.stack([jnp.cos(f0), jnp.sin(f0), jnp.cos(f1), jnp.sin(f1)])
    polar, azimuth = stencils(tap_u, weight_u, trig, tap_v, weight_v)
    arrived, table5, src5, off5, src4, off4, polar, azimuth, tab = lax.optimization_barrier(
        (arrived, table5, src5, off5, src4, off4, polar, azimuth, tab)
    )

    level = arrived.reshape(64, 128, 128)
    right, left, last, first = edges(level)
    around = lambda step: [(i, (i + step) % blocks) for i in range(blocks)]
    across = lambda step: [(i, i + step) for i in range(bands) if 0 <= i + step < bands]
    from_left = lax.ppermute(right, "clu", around(1))
    from_right = lax.ppermute(left, "clu", around(-1))
    low = lax.ppermute(last, "ang", across(1))
    high = lax.ppermute(first, "ang", across(-1))
    translated5 = translate5(arrived.reshape(512, 16, 128), table5, src5, off5)
    from_left, from_right, translated5 = lax.optimization_barrier(
        (from_left, from_right, translated5)
    )
    sides, side_last, side_first = corners(from_left, from_right)
    side_low = lax.ppermute(side_last, "ang", across(1))
    side_high = lax.ppermute(side_first, "ang", across(-1))
    half = theta_level(level, low, high, polar)
    translated4 = top_level(
        half, sides, side_low, side_high, polar, azimuth, tab, transfer4, src4, off4
    )
    return (translated5, translated4)


def solution(mesh):
    in_specs = (
        P(("clu", "ang"), None, None, None),
        P(),
        P(),
        P(),
        P(),
        P(),
        P(),
        P(),
        P(),
        P(None, None, "ang", "clu"),
        P(),
        P(),
        P(None, None, "ang", "clu"),
        P(),
        P(),
    )
    out_specs = (P(None, None, "ang", "clu"), P(None, None, "ang", "clu"))
    return jax.shard_map(shards, mesh=mesh, in_specs=in_specs, out_specs=out_specs, check_vma=False)
```

```python
import math

import jax
import jax.numpy as jnp
import numpy as np
from jax import lax
from jax.experimental import pallas as pl
from jax.experimental.pallas import tpu as pltpu
from jax.sharding import PartitionSpec as P

F32 = jnp.float32
BF16 = jnp.bfloat16


PAIRS = ((3, 0), (1, 2))


def theta_phase(rows):
    return rows / 8.0 * np.cos(np.pi * (np.arange(rows) + 0.5) / rows)


def plane_phases(rows, cols, count):
    theta = np.pi * (np.arange(rows) + 0.5) / rows
    phi = 2.0 * np.pi * np.arange(count) / cols
    x = np.sin(theta)[:, None] * np.cos(phi)[None, :]
    y = np.sin(theta)[:, None] * np.sin(phi)[None, :]
    return rows / 8.0 * (x + y), rows / 8.0 * (x - y)


def fold_factors(rows, inner):
    phase = theta_phase(rows)[:, None]
    cosine = np.broadcast_to(np.cos(phase), (rows, inner))
    sine = np.broadcast_to(np.sin(phase), (rows, inner))
    top = np.concatenate([cosine, sine, cosine, -sine], axis=1)
    bottom = np.concatenate([-sine, cosine, sine, cosine], axis=1)
    return top.astype(np.float32), bottom.astype(np.float32)


def dot(a, b):
    return jnp.dot(a, b, preferred_element_type=F32)


def dot_t(a, b):
    return lax.dot_general(a, b, (((1,), (1,)), ((), ())), preferred_element_type=F32)


def aggregate_body(
    pat, a7, b7, a6, b6, top7, bottom7, cz, sz, tab6, tab5, out, m7, m6, level6, mixed, half6
):
    rows7, rows6, rows5 = a7.shape[0], a7.shape[1], a6.shape[0]
    cols6, cols5 = b7.shape[1], b6.shape[1]

    @pl.when(pl.program_id(0) == 0)
    def _():
        src = lax.broadcasted_iota(jnp.int32, (rows7, 4 * rows7), 0)
        dst = lax.broadcasted_iota(jnp.int32, (rows7, 4 * rows7), 1)
        spread = jnp.where((dst & (rows7 - 1)) == src, 1.0, 0.0).astype(BF16)
        wide = lax.dot_general(
            a7[...], spread, (((0,), (0,)), ((), ())), preferred_element_type=F32
        )
        m7[0:rows6, :] = (wide * top7[...]).astype(BF16)
        m7[rows6 : 2 * rows6, :] = (wide * bottom7[...]).astype(BF16)
        base = a6[...].astype(F32)
        c = base * cz[...]
        s = base * sz[...]
        m6[0, :, 0:rows6] = c.astype(BF16)
        m6[0, :, rows6 : 2 * rows6] = (-s).astype(BF16)
        m6[1, :, 0:rows6] = c.astype(BF16)
        m6[1, :, rows6 : 2 * rows6] = s.astype(BF16)

    step = 2 * rows7
    for o6 in range(8):
        base = o6 * 8 * step
        parts = []
        for k in range(4):
            low = pat[base + k * step : base + (k + 1) * step, :]
            high = pat[base + (k + 4) * step : base + (k + 5) * step, :]
            parts.append(jnp.concatenate([low, high], axis=0))
        lanes = parts[0].shape[1]
        h = dot(m7[...], jnp.concatenate(parts, axis=1))
        rows = []
        for a, b in PAIRS:
            ya = h[:, a * lanes : (a + 1) * lanes]
            yb = h[:, b * lanes : (b + 1) * lanes]
            rows.append((ya + yb).astype(BF16))
            rows.append((ya - yb).astype(BF16))
        y = dot(jnp.concatenate(rows, axis=0), b7[...])
        for half in range(2):
            cols = slice(half * (cols6 // 2), (half + 1) * (cols6 // 2))
            re = None
            for q in range(2):
                at = q * 4 * rows6
                pr = y[at : at + rows6, cols]
                pi = y[at + rows6 : at + 2 * rows6, cols]
                qr = y[at + 2 * rows6 : at + 3 * rows6, cols]
                qi = y[at + 3 * rows6 : at + 4 * rows6, cols]
                c = tab6[2 * q]
                s = tab6[2 * q + 1]
                if half == 1:
                    dr = c * pr + s * qi
                    di = c * pi - s * qr
                else:
                    dr = c * pr - s * qi
                    di = c * pi + s * qr
                re, im = (dr, di) if re is None else (re + dr, im + di)
            level6[o6, 0, :, cols] = re
            level6[o6, 1, :, cols] = im

    for part in range(2):
        for r in range(0, rows6, 16):
            x = [level6[o, part, r : r + 16, :] for o in range(8)]
            for t in range(2):
                z = [x[k + 4] + x[k] if t == 0 else x[k + 4] - x[k] for k in range(4)]
                for q, (a, b) in enumerate(PAIRS):
                    mixed[2 * q, t, part, r : r + 16, :] = (z[a] + z[b]).astype(BF16)
                    mixed[2 * q + 1, t, part, r : r + 16, :] = (z[a] - z[b]).astype(BF16)

    for x in range(4):
        for part in range(2):
            rhs = jnp.concatenate([mixed[x, 0, part], mixed[x, 1, 1 - part]], axis=0)
            half6[x, part] = dot(m6[part], rhs).astype(BF16)

    block = 64
    quarter = cols5 // 4
    low_lane = lax.broadcasted_iota(jnp.int32, (block, quarter), 1) < quarter // 2
    for u in range(0, rows5, block):
        lhs = jnp.concatenate(
            [half6[x, part, u : u + block, :] for x in range(4) for part in range(2)], axis=0
        )
        y = dot(lhs, b6[...])
        for tile in range(4):
            cols = slice(tile * quarter, (tile + 1) * quarter)
            re = None
            for q in range(2):
                at = q * 4 * block
                pr = y[at : at + block, cols]
                pi = y[at + block : at + 2 * block, cols]
                qr = y[at + 2 * block : at + 3 * block, cols]
                qi = y[at + 3 * block : at + 4 * block, cols]
                place = (tile + q) % 4
                c = tab5[place % 2, 0, u : u + block, :]
                s = tab5[place % 2, 1, u : u + block, :]
                if place >= 2:
                    dr = c * pr + s * qi
                    di = c * pi - s * qr
                else:
                    dr = c * pr - s * qi
                    di = c * pi + s * qr
                if q == 0:
                    re, im = dr, di
                else:
                    re, im = re + dr, im + di
            if_low = jnp.where(low_lane, re, pltpu.roll(im, quarter // 2, 1)).astype(BF16)
            if_high = jnp.where(low_lane, pltpu.roll(re, quarter // 2, 1), im).astype(BF16)
            for r in range(0, block, 16):
                band = (u + r) // 16
                out[2 * tile * 16 + band, 0] = if_low[r : r + 16, :]
                out[(2 * tile + 1) * 16 + band, 0] = if_high[r : r + 16, :]


def aggregate(patterns7, polar_up7, azimuth_up7, polar_up6, azimuth_up6):
    children, _, rows7, cols7 = patterns7.shape
    rows6, rows5 = polar_up7.shape[0], polar_up6.shape[0]
    cols6, cols5 = azimuth_up7.shape[1], azimuth_up6.shape[1]
    clusters = children // 64
    pat = patterns7.reshape(children * 2 * rows7, cols7)
    top7, bottom7 = fold_factors(rows6, rows7)
    z = theta_phase(rows5)[:, None]
    cz = np.broadcast_to(np.cos(z), (rows5, rows6)).astype(np.float32)
    sz = np.broadcast_to(np.sin(z), (rows5, rows6)).astype(np.float32)
    f0, f1 = plane_phases(rows6, cols6, cols6 // 2)
    tab6 = np.stack([np.cos(f0), np.sin(f0), np.cos(f1), np.sin(f1)]).astype(np.float32)
    g0, _ = plane_phases(rows5, cols5, cols5 // 2)
    g0 = g0.reshape(rows5, 2, cols5 // 4).transpose(1, 0, 2)
    tab5 = np.stack([np.cos(g0), np.sin(g0)], axis=1).astype(np.float32)
    full = lambda shape: pl.BlockSpec(shape, lambda g: (0,) * len(shape))
    consts = (top7, bottom7, cz, sz, tab6, tab5)
    weights = (polar_up7.T, azimuth_up7, polar_up6, azimuth_up6)
    lines = pat.shape[0] // clusters
    return pl.pallas_call(
        aggregate_body,
        grid=(clusters,),
        in_specs=[pl.BlockSpec((lines, cols7), lambda g: (g, 0))]
        + [full(a.shape) for a in weights]
        + [full(a.shape) for a in consts],
        out_specs=pl.BlockSpec((128, 1, 16, 128), lambda g: (0, g, 0, 0)),
        out_shape=jax.ShapeDtypeStruct((128, clusters, 16, 128), BF16),
        scratch_shapes=[
            pltpu.VMEM((2 * rows6, 4 * rows7), BF16),
            pltpu.VMEM((2, rows5, 2 * rows6), BF16),
            pltpu.VMEM((8, 2, rows6, cols6), F32),
            pltpu.VMEM((4, 2, 2, rows6, cols6), BF16),
            pltpu.VMEM((4, 2, rows5, cols6), BF16),
        ],
        compiler_params=pltpu.CompilerParams(vmem_limit_bytes=58 * 1024 * 1024),
        name="aggregate",
    )(pat, *weights, *[jnp.asarray(a) for a in consts])


def table_body(tr, out):
    theta = pl.program_id(0)
    entries = out.shape[0] // 16
    count = tr.shape[4]
    stack = jnp.concatenate([tr[0, 0, 0], tr[0, 1, 0], tr[1, 0, 0], tr[1, 1, 0]], axis=0)
    row = lax.broadcasted_iota(jnp.int32, (entries, count), 0)
    col = lax.broadcasted_iota(jnp.int32, (entries, count), 1)
    unit = jnp.where(row == col, 1.0, 0.0).astype(BF16)
    turned = dot_t(unit, stack)
    out[pl.ds(theta, entries, 16), :] = turned[:, :128]
    out[pl.ds(theta + 8, entries, 16), :] = turned[:, 128:]


def transfer_table(transfer):
    count, _, rows, cols = transfer.shape
    entries = (count + 1 + 7) // 8 * 8
    turned = transfer.transpose(1, 2, 3, 0).reshape(2, 2, rows // 2, cols, count)
    return pl.pallas_call(
        table_body,
        grid=(rows // 2,),
        in_specs=[pl.BlockSpec((2, 2, 1, cols, count), lambda i: (0, 0, i, 0, 0))],
        out_specs=pl.BlockSpec((entries * 16, 128), lambda i: (0, 0)),
        out_shape=jax.ShapeDtypeStruct((entries * 16, 128), F32),
        compiler_params=pltpu.CompilerParams(vmem_limit_bytes=12 * 1024 * 1024),
        name="transfer_table",
    )(turned)


def tree(terms):
    while len(terms) > 1:
        rest = terms[len(terms) // 2 * 2 :]
        terms = [terms[i] + terms[i + 1] for i in range(0, len(terms) - 1, 2)] + rest
    return terms[0]


def by_class(order, starts, slots, group, one):
    for index, count in enumerate(slot_classes(slots)):
        begin, end = starts[index], starts[index + 1]

        def some(i, carry, begin=begin, end=end, count=count):
            for k in range(group):
                one(order[jnp.minimum(begin + i * group + k, end - 1)], count)
            return carry

        lax.fori_loop(0, (end - begin + group - 1) // group, some, 0)


def slot_classes(slots):
    return tuple(range(slots // 2, slots + 1, 2))


def target_classes(sources):
    targets, slots = sources.shape
    live = jnp.sum((sources >= 0).astype(jnp.int32), axis=1)
    kind = sum((live > count).astype(jnp.int32) for count in slot_classes(slots)[:-1])
    index = jnp.arange(targets, dtype=jnp.int32)
    key = kind * targets + index
    place = jnp.sum((key[None, :] < key[:, None]).astype(jnp.int32), axis=1)
    order = jnp.sum(jnp.where(place[None, :] == index[:, None], index[None, :], 0), axis=1)
    kinds = jnp.arange(len(slot_classes(slots)) + 1, dtype=jnp.int32)
    starts = jnp.sum((kind[None, :] < kinds[:, None]).astype(jnp.int32), axis=1)
    return order, starts


def translate_targets(src, off, order, starts, tiles, table, total, out):
    targets, lanes = order.shape[0], tiles.shape[1]
    slots = src.shape[0] // targets

    def one(t, count):
        terms_r, terms_i = [], []
        for j in range(count):
            s = pl.multiple_of(src[t * slots + j], 16)
            o = pl.multiple_of(off[t * slots + j], 16)
            xr = tiles[pl.ds(s, 8), :]
            xi = tiles[pl.ds(s + 8, 8), :]
            wr = table[pl.ds(o, 8), :]
            wi = table[pl.ds(o + 8, 8), :]
            terms_r.append(wr * xr - wi * xi)
            terms_i.append(wr * xi + wi * xr)
        at = pl.multiple_of(t * 16, 16)
        total[pl.ds(at, 8), :] = tree(terms_r)
        total[pl.ds(at + 8, 8), :] = tree(terms_i)

    by_class(order, starts, slots, 4, one)
    unit = jnp.where(
        lax.broadcasted_iota(jnp.int32, (lanes, lanes), 0)
        == lax.broadcasted_iota(jnp.int32, (lanes, lanes), 1),
        1.0,
        0.0,
    ).astype(BF16)
    for row in range(16):
        turned = dot_t(unit, total[pl.ds(row, targets, 16), :].astype(BF16)).astype(BF16)
        out[row // 8, row % 8] = turned[: lanes // 2]
        out[row // 8, row % 8 + 8] = turned[lanes // 2 :]


def first_targets_body(src, off, order, starts, level, table_from, out, tiles, table, total, sem):
    clusters, rows, lanes = level.shape
    low = lax.broadcasted_iota(jnp.int32, (8, lanes), 1) < lanes // 2
    fetch = pltpu.make_async_copy(table_from, table, sem)
    fetch.start()

    def widen(t, carry):
        x = level[t].astype(F32)
        upper, lower = x[:8], x[8:]
        at = pl.multiple_of(t * 16, 16)
        tiles[pl.ds(at, 8), :] = jnp.where(low, upper, pltpu.roll(lower, lanes // 2, 1))
        tiles[pl.ds(at + 8, 8), :] = jnp.where(low, pltpu.roll(upper, lanes // 2, 1), lower)
        return carry

    lax.fori_loop(0, clusters, widen, 0, unroll=16)
    fetch.wait()
    translate_targets(src, off, order, starts, tiles, table, total, out)


def last_targets_body(
    src, off, order, starts, tiles, table, before, out, total, turned, sem_before, sem_after
):
    targets = order.shape[0]
    pass_on = pltpu.make_async_copy(before, out.at[:, :, :, pl.ds(0, targets)], sem_before)
    pass_on.start()
    translate_targets(src, off, order, starts, tiles, table, total, turned)
    finish = pltpu.make_async_copy(turned, out.at[:, :, :, pl.ds(targets, targets)], sem_after)
    finish.start()
    finish.wait()
    pass_on.wait()


SMEM_SPEC = pl.BlockSpec(memory_space=pltpu.SMEM)
VMEM_SPEC = pl.BlockSpec(memory_space=pltpu.VMEM)
ANY_SPEC = pl.BlockSpec(memory_space=pl.ANY)


def translate_first(level, table, lists):
    clusters, rows, lanes = level.shape
    targets = lists[2].shape[0]
    return pl.pallas_call(
        first_targets_body,
        in_specs=[SMEM_SPEC] * 4 + [VMEM_SPEC, pl.BlockSpec(memory_space=pltpu.HBM)],
        out_specs=(VMEM_SPEC,) * 3,
        out_shape=(
            jax.ShapeDtypeStruct((2, rows, lanes // 2, targets), BF16),
            jax.ShapeDtypeStruct((clusters * 16, lanes), F32),
            jax.ShapeDtypeStruct(table.shape, F32),
        ),
        scratch_shapes=[pltpu.VMEM((targets * 16, lanes), F32), pltpu.SemaphoreType.DMA],
        compiler_params=pltpu.CompilerParams(vmem_limit_bytes=20 * 1024 * 1024),
        name="translate_first",
    )(*lists, level, table)


def translate_last(tiles, table, before, lists):
    parts, rows, half, targets = before.shape
    turned = pl.pallas_call(
        last_targets_body,
        in_specs=[SMEM_SPEC] * 4 + [VMEM_SPEC] * 3,
        out_specs=ANY_SPEC,
        out_shape=jax.ShapeDtypeStruct((parts, rows, half, 2 * targets), BF16),
        scratch_shapes=[
            pltpu.VMEM((targets * 16, tiles.shape[1]), F32),
            pltpu.VMEM(before.shape, BF16),
            pltpu.SemaphoreType.DMA,
            pltpu.SemaphoreType.DMA,
        ],
        compiler_params=pltpu.CompilerParams(vmem_limit_bytes=20 * 1024 * 1024),
        name="translate_last",
    )(*lists, tiles, table, before)
    return turned.transpose(3, 0, 1, 2)


def edge_picks():
    pick = np.zeros((96, 256), np.float32)
    for side in range(2):
        for n in range(48):
            parent, child, j = n // 24, n % 24 // 3, n % 3
            pick[side * 48 + n, parent * 128 + child * 16 + (13 if side == 0 else 0) + j] = 1.0
    return pick


def edge_columns_body(level, right, left):
    lane = lax.broadcasted_iota(jnp.int32, (1024, 256), 0)
    col = lax.broadcasted_iota(jnp.int32, (1024, 256), 1)
    side = col >> 7
    place = lane >> 7
    part = (lane >> 6) & 1
    j = col & 3
    hit = (
        (((col & 127) >> 4) == place)
        & (((col >> 3) & 1) == side)
        & (((col >> 2) & 1) == part)
        & (j < 3)
        & ((lane & 63) == jnp.where(side == 0, 61 + j, j))
    )
    spread = jnp.where(hit, 1.0, 0.0).astype(BF16)
    for g in range(8):
        lhs = jnp.concatenate([level[8 * g + i] for i in range(8)], axis=1)
        both = dot(lhs, spread).astype(BF16)
        right[g] = both[:, :128]
        left[g] = both[:, 128:]


def edge_columns(level):
    return pl.pallas_call(
        edge_columns_body,
        out_shape=(jax.ShapeDtypeStruct((8, 128, 128), BF16),) * 2,
        compiler_params=pltpu.CompilerParams(vmem_limit_bytes=10 * 1024 * 1024),
        name="edge_columns",
    )(level)


def edge_rows_body(level, from_left, from_right, pick, sides, last, first):
    for g in range(sides.shape[0]):
        sides[g] = from_left[g] + from_right[g]
    own = level.shape[0] // 2
    for i in range(last.shape[0]):
        source, at = (level, 2 * i) if i < own else (sides, 2 * (i - own))
        both = dot(pick[...], jnp.concatenate([source[at], source[at + 1]], axis=0)).astype(BF16)
        last[i] = both[:48]
        first[i] = both[48:]


def edge_rows(level, from_left, from_right):
    pairs = (level.shape[0] + from_left.shape[0]) // 2
    return pl.pallas_call(
        edge_rows_body,
        out_shape=(jax.ShapeDtypeStruct(from_left.shape, BF16),)
        + (jax.ShapeDtypeStruct((pairs, 48, 128), BF16),) * 2,
        compiler_params=pltpu.CompilerParams(vmem_limit_bytes=8 * 1024 * 1024),
        name="edge_rows",
    )(level, from_left, from_right, jnp.asarray(edge_picks(), BF16))


def stencil_maps():
    ext = np.zeros((1, 224), np.int32)
    factor = np.zeros((2, 8, 224), np.float32)
    sign = np.zeros((4, 8))
    for q, (a, b) in enumerate(PAIRS):
        for h in range(2):
            sign[2 * q, a + 4 * h] = sign[2 * q, b + 4 * h] = 1.0
            sign[2 * q + 1, a + 4 * h] = 1.0
            sign[2 * q + 1, b + 4 * h] = -1.0
    for col in range(224):
        if col < 128:
            owner, child, ext[0, col] = (0, 1), col // 16, col % 16 + 3
        else:
            n = (col - 128) % 48
            owner, child = (n // 24,), n % 24 // 3
            ext[0, col] = n % 3 + (0 if col < 176 else 19)
        for parity in owner:
            for x in range(4):
                factor[parity, 2 * x, col] = sign[x, child]
                factor[parity, 2 * x + 1, col] = sign[x, child] * (1.0 if child >= 4 else -1.0)
    return ext, factor


def stencils_body(tap_u, weight_u, trig, tap_v, weight_v, ext, factor, polar, azimuth):
    rows = tap_u.shape[0]
    base = jnp.zeros((rows, ext.shape[1]), F32)
    for k in range(4):
        base = base + jnp.where(tap_u[:, k : k + 1] == ext[...], weight_u[:, k : k + 1], 0.0)
    for parity in range(2):
        for kind in range(8):
            turned = base * trig[:, kind % 2 : kind % 2 + 1]
            polar[parity, kind * rows : (kind + 1) * rows, :] = (
                turned * factor[parity, kind : kind + 1, :]
            ).astype(BF16)
    i = lax.broadcasted_iota(jnp.int32, (128, 128), 0)

    def fill(at, matrix, part, index):
        first = part == 0
        azimuth[index, at : at + 128, :128] = jnp.where(first, matrix, 0.0).astype(BF16)
        azimuth[index, at : at + 128, 128:] = jnp.where(first, 0.0, matrix).astype(BF16)
        azimuth[index, at + 128 : at + 256, :128] = jnp.where(first, 0.0, -matrix).astype(BF16)
        azimuth[index, at + 128 : at + 256, 128:] = jnp.where(first, matrix, 0.0).astype(BF16)

    def matrix_at(q):
        total = jnp.zeros((128, 128), F32)
        for k in range(4):
            total = total + jnp.where(tap_v[k : k + 1, :] == q, weight_v[k : k + 1, :], 0.0)
        return total

    own = matrix_at((i & 63) + 3)
    j = i & 3
    halo = jnp.where(j < 3, matrix_at(j + 67 * ((i >> 3) & 1)), 0.0)
    for index in range(8):
        fill(0, own, i >> 6, index)
        fill(256, jnp.where((i >> 4) == index, halo, 0.0), (i >> 2) & 1, index)


def stencils(tap_u, weight_u, trig, tap_v, weight_v):
    ext, factor = stencil_maps()
    rows = tap_u.shape[0]
    return pl.pallas_call(
        stencils_body,
        out_shape=(
            jax.ShapeDtypeStruct((2, 8 * rows, 224), BF16),
            jax.ShapeDtypeStruct((8, 512, 256), BF16),
        ),
        compiler_params=pltpu.CompilerParams(vmem_limit_bytes=8 * 1024 * 1024),
        name="stencils",
    )(tap_u, weight_u, trig, tap_v, weight_v, jnp.asarray(ext), jnp.asarray(factor))


def theta_stage(level, low, high, at, polar, half):
    for i in range(level.shape[0] // 2):
        for parity in range(2):
            rhs = jnp.concatenate([level[2 * i + parity], low[at + i], high[at + i]], axis=0)
            half[2 * i + parity] = dot(polar[parity], rhs).astype(BF16)


def top_body(
    src, off, order, starts, level, sides, low, high, polar, azimuth, tab, transfer, out,
    table, half, side_half, level4, sem,
):
    count = transfer.shape[0]
    fetch = pltpu.make_async_copy(transfer, table.at[pl.ds(0, count)], sem)
    fetch.start()
    table[count] = jnp.zeros(table.shape[1:], BF16)
    theta_stage(level, low, high, 0, polar, half)
    theta_stage(sides, low, high, level.shape[0] // 2, polar, side_half)

    def phi_stage(place, carry):
        rows = []
        for g in range(8):
            for x in range(4):
                a = slice(64 * x, 64 * x + 32)
                b = slice(64 * x + 32, 64 * x + 64)
                p = 8 * g + place
                rows.append(
                    jnp.concatenate([half[p, a], half[p, b], side_half[g, a], side_half[g, b]], axis=1)
                )
        y = dot(jnp.concatenate(rows, axis=0), azimuth[place])
        for g in range(8):
            re = im = None
            for q in range(2):
                at = 128 * g + 64 * q
                pr = y[at : at + 32, :128]
                pi = y[at : at + 32, 128:]
                qr = y[at + 32 : at + 64, :128]
                qi = y[at + 32 : at + 64, 128:]
                c = tab[2 * q]
                s = tab[2 * q + 1]
                dr = c * pr - s * qi
                di = c * pi + s * qr
                re, im = (dr, di) if q == 0 else (re + dr, im + di)
            at = pl.multiple_of((8 * g + place) * 64, 64)
            level4[pl.ds(at, 32), :] = re
            level4[pl.ds(at + 32, 32), :] = im
        return carry

    lax.fori_loop(0, 8, phi_stage, 0)
    fetch.wait()
    targets = out.shape[0]
    slots = src.shape[0] // targets

    def one(t, count):
        re = [jnp.zeros((8, 128), F32)] * 4
        im = [jnp.zeros((8, 128), F32)] * 4
        for j in range(count):
            at = pl.multiple_of(src[t * slots + j], 64)
            w = table.at[off[t * slots + j]]
            for r in range(4):
                xr = level4[pl.ds(at + 8 * r, 8), :]
                xi = level4[pl.ds(at + 32 + 8 * r, 8), :]
                wr = w[0, 8 * r : 8 * r + 8].astype(F32)
                wi = w[1, 8 * r : 8 * r + 8].astype(F32)
                re[r] = re[r] + (wr * xr - wi * xi)
                im[r] = im[r] + (wr * xi + wi * xr)
        for r in range(4):
            out[t, 0, 8 * r : 8 * r + 8] = re[r].astype(BF16)
            out[t, 1, 8 * r : 8 * r + 8] = im[r].astype(BF16)

    by_class(order, starts, slots, 1, one)


def top_level(level, sides, low, high, polar, azimuth, tab, transfer, sources, offsets, order, starts):
    count, _, rows, cols = transfer.shape
    parents = level.shape[0]
    lines = polar.shape[1:2] + level.shape[2:]
    return pl.pallas_call(
        top_body,
        in_specs=[SMEM_SPEC] * 4 + [VMEM_SPEC] * 7 + [ANY_SPEC],
        out_specs=VMEM_SPEC,
        out_shape=jax.ShapeDtypeStruct((parents, 2, rows, cols), BF16),
        scratch_shapes=[
            pltpu.VMEM((count + 1, 2, rows, cols), BF16),
            pltpu.VMEM((parents,) + lines, BF16),
            pltpu.VMEM((sides.shape[0],) + lines, BF16),
            pltpu.VMEM((parents * 2 * rows, cols), F32),
            pltpu.SemaphoreType.DMA,
        ],
        compiler_params=pltpu.CompilerParams(vmem_limit_bytes=24 * 1024 * 1024),
        name="top_level",
    )(sources, offsets, order, starts, level, sides, low, high, polar, azimuth, tab, transfer)


def flat_lists(sources, offsets, dead, source_rows, factor_rows):
    src = jnp.maximum(sources, 0) * source_rows
    off = jnp.where(offsets < 0, dead, offsets) * factor_rows
    return (src.reshape(-1), off.reshape(-1)) + target_classes(sources)


def shards(
    patterns7,
    polar_up7,
    azimuth_up7,
    polar_up6,
    azimuth_up6,
    polar_first,
    polar_weights,
    azimuth_first,
    azimuth_weights,
    transfer5,
    sources5,
    offsets5,
    transfer4,
    sources4,
    offsets4,
):
    bands = lax.axis_size("ang")
    blocks = lax.axis_size("clu")
    band = lax.axis_index("ang")
    block = lax.axis_index("clu")

    send = aggregate(patterns7, polar_up7, azimuth_up7, polar_up6, azimuth_up6)
    arrived = lax.all_to_all(send, ("clu", "ang"), split_axis=0, concat_axis=0, tiled=True)

    count5 = transfer5.shape[0]
    count4 = transfer4.shape[0]
    table5 = transfer_table(transfer5)
    half5 = sources5.shape[0] // 2
    lists5 = (
        flat_lists(sources5[:half5], offsets5[:half5], count5, 16, 16),
        flat_lists(sources5[half5:], offsets5[half5:], count5, 16, 16),
    )
    lists4 = flat_lists(sources4, offsets4, count4, 64, 1)
    rows4 = polar_first.shape[0]
    cols4 = azimuth_first.shape[0]
    band_rows = rows4 // bands
    block_cols = cols4 // blocks
    taps = jnp.arange(4, dtype=jnp.int32)
    tap_u = lax.dynamic_slice_in_dim(polar_first, band * band_rows, band_rows, 0)
    tap_u = (tap_u - band * (band_rows // 2) + 3)[:, None] + taps[None, :]
    weight_u = lax.dynamic_slice_in_dim(polar_weights, band * band_rows, band_rows, 0).astype(F32)
    tap_v = lax.dynamic_slice_in_dim(azimuth_first, block * block_cols, block_cols, 0)
    tap_v = (tap_v[None, :] + taps[:, None] - block * (block_cols // 2) + 3) % (cols4 // 2)
    weight_v = lax.dynamic_slice_in_dim(azimuth_weights, block * block_cols, block_cols, 0)
    weight_v = weight_v.T.astype(F32)
    theta = (jnp.arange(band_rows, dtype=jnp.int32) + band * band_rows).astype(F32)
    theta = (theta + 0.5) * (math.pi / rows4)
    phi = (jnp.arange(block_cols, dtype=jnp.int32) + block * block_cols).astype(F32)
    phi = phi * (2.0 * math.pi / cols4)
    scale = rows4 / 8.0
    lift = scale * jnp.cos(theta)
    trig = jnp.stack([jnp.cos(lift), jnp.sin(lift)], axis=1)
    x = jnp.sin(theta)[:, None] * jnp.cos(phi)[None, :]
    y = jnp.sin(theta)[:, None] * jnp.sin(phi)[None, :]
    f0 = scale * (x + y)
    f1 = scale * (x - y)
    tab = jnp.stack([jnp.cos(f0), jnp.sin(f0), jnp.cos(f1), jnp.sin(f1)])
    polar, azimuth = stencils(tap_u, weight_u, trig, tap_v, weight_v)
    arrived, table5, lists5, lists4, polar, azimuth, tab = lax.optimization_barrier(
        (arrived, table5, lists5, lists4, polar, azimuth, tab)
    )

    level = arrived.reshape(64, 128, 128)
    right, left = edge_columns(level)
    around = lambda step: [(i, (i + step) % blocks) for i in range(blocks)]
    across = lambda step: [(i, i + step) for i in range(bands) if 0 <= i + step < bands]
    from_left = lax.ppermute(right, "clu", around(1))
    from_right = lax.ppermute(left, "clu", around(-1))
    before, tiles, table5 = translate_first(arrived.reshape(512, 16, 128), table5, lists5[0])
    from_left, from_right, tiles = lax.optimization_barrier((from_left, from_right, tiles))
    sides, last, first = edge_rows(level, from_left, from_right)
    last, first, tiles = lax.optimization_barrier((last, first, tiles))
    low = lax.ppermute(last, "ang", across(1))
    high = lax.ppermute(first, "ang", across(-1))
    translated5 = translate_last(tiles, table5, before, lists5[1])
    translated4 = top_level(
        level, sides, low, high, polar, azimuth, tab, transfer4, *lists4
    )
    return (translated5, translated4)


def solution(mesh):
    in_specs = (
        P(("clu", "ang"), None, None, None),
        P(),
        P(),
        P(),
        P(),
        P(),
        P(),
        P(),
        P(),
        P(None, None, "ang", "clu"),
        P(),
        P(),
        P(None, None, "ang", "clu"),
        P(),
        P(),
    )
    out_specs = (P(None, None, "ang", "clu"), P(None, None, "ang", "clu"))
    return jax.shard_map(shards, mesh=mesh, in_specs=in_specs, out_specs=out_specs, check_vma=False)
```

```python
import math

import jax
import jax.numpy as jnp
import numpy as np
from jax import lax
from jax.experimental import pallas as pl
from jax.experimental.pallas import tpu as pltpu
from jax.sharding import PartitionSpec as P

F32 = jnp.float32
BF16 = jnp.bfloat16
TOGETHER = 2
BLOCK5 = 128


PAIRS = ((3, 0), (1, 2))


def theta_phase(rows):
    return rows / 8.0 * np.cos(np.pi * (np.arange(rows) + 0.5) / rows)


def plane_phases(rows, cols, count):
    theta = np.pi * (np.arange(rows) + 0.5) / rows
    phi = 2.0 * np.pi * np.arange(count) / cols
    x = np.sin(theta)[:, None] * np.cos(phi)[None, :]
    y = np.sin(theta)[:, None] * np.sin(phi)[None, :]
    return rows / 8.0 * (x + y), rows / 8.0 * (x - y)


def fold_factors(rows, inner):
    phase = theta_phase(rows)[:, None]
    cosine = np.broadcast_to(np.cos(phase), (rows, inner))
    sine = np.broadcast_to(np.sin(phase), (rows, inner))
    top = np.concatenate([cosine, sine, cosine, -sine], axis=1)
    bottom = np.concatenate([-sine, cosine, sine, cosine], axis=1)
    return top.astype(np.float32), bottom.astype(np.float32)


def dot(a, b):
    return jnp.dot(a, b, preferred_element_type=F32)


def dot_t(a, b):
    return lax.dot_general(a, b, (((1,), (1,)), ((), ())), preferred_element_type=F32)


def aggregate_body(
    pat, a7, b7, a6, b6, top7, bottom7, cz, sz, tab6, tab5, out, m7, m6, level6, mixed, half6
):
    rows7, rows6, rows5 = a7.shape[0], a7.shape[1], a6.shape[0]
    cols6, cols5 = b7.shape[1], b6.shape[1]

    @pl.when(pl.program_id(0) == 0)
    def _():
        src = lax.broadcasted_iota(jnp.int32, (rows7, 4 * rows7), 0)
        dst = lax.broadcasted_iota(jnp.int32, (rows7, 4 * rows7), 1)
        spread = jnp.where((dst & (rows7 - 1)) == src, 1.0, 0.0).astype(BF16)
        wide = lax.dot_general(
            a7[...], spread, (((0,), (0,)), ((), ())), preferred_element_type=F32
        )
        m7[0:rows6, :] = (wide * top7[...]).astype(BF16)
        m7[rows6 : 2 * rows6, :] = (wide * bottom7[...]).astype(BF16)
        base = a6[...].astype(F32)
        c = base * cz[...]
        s = base * sz[...]
        m6[0, :, 0:rows6] = c.astype(BF16)
        m6[0, :, rows6 : 2 * rows6] = (-s).astype(BF16)
        m6[1, :, 0:rows6] = c.astype(BF16)
        m6[1, :, rows6 : 2 * rows6] = s.astype(BF16)

    step = 2 * rows7
    for first in range(0, 8, TOGETHER):
        stacks = []
        for o6 in range(first, first + TOGETHER):
            base = o6 * 8 * step
            for k in range(4):
                low = pat[base + k * step : base + (k + 1) * step, :]
                high = pat[base + (k + 4) * step : base + (k + 5) * step, :]
                stacks.append(jnp.concatenate([low, high], axis=0))
        lanes = stacks[0].shape[1]
        h = dot(m7[...], jnp.concatenate(stacks, axis=1))
        rows = []
        for n in range(TOGETHER):
            for a, b in PAIRS:
                ya = h[:, (4 * n + a) * lanes : (4 * n + a + 1) * lanes]
                yb = h[:, (4 * n + b) * lanes : (4 * n + b + 1) * lanes]
                rows.append((ya + yb).astype(BF16))
                rows.append((ya - yb).astype(BF16))
        everything = dot(jnp.concatenate(rows, axis=0), b7[...])
        for n in range(TOGETHER):
            y = everything[n * 8 * rows6 : (n + 1) * 8 * rows6]
            for half in range(2):
                cols = slice(half * (cols6 // 2), (half + 1) * (cols6 // 2))
                re = None
                for q in range(2):
                    at = q * 4 * rows6
                    pr = y[at : at + rows6, cols]
                    pi = y[at + rows6 : at + 2 * rows6, cols]
                    qr = y[at + 2 * rows6 : at + 3 * rows6, cols]
                    qi = y[at + 3 * rows6 : at + 4 * rows6, cols]
                    c = tab6[2 * q]
                    s = tab6[2 * q + 1]
                    if half == 1:
                        dr = c * pr + s * qi
                        di = c * pi - s * qr
                    else:
                        dr = c * pr - s * qi
                        di = c * pi + s * qr
                    re, im = (dr, di) if re is None else (re + dr, im + di)
                level6[first + n, 0, :, cols] = re
                level6[first + n, 1, :, cols] = im

    for part in range(2):
        for r in range(0, rows6, 16):
            x = [level6[o, part, r : r + 16, :] for o in range(8)]
            for t in range(2):
                z = [x[k + 4] + x[k] if t == 0 else x[k + 4] - x[k] for k in range(4)]
                for q, (a, b) in enumerate(PAIRS):
                    mixed[2 * q, t, part, r : r + 16, :] = (z[a] + z[b]).astype(BF16)
                    mixed[2 * q + 1, t, part, r : r + 16, :] = (z[a] - z[b]).astype(BF16)

    for x in range(4):
        for part in range(2):
            rhs = jnp.concatenate([mixed[x, 0, part], mixed[x, 1, 1 - part]], axis=0)
            half6[x, part] = dot(m6[part], rhs).astype(BF16)

    block = BLOCK5
    quarter = cols5 // 4
    low_lane = lax.broadcasted_iota(jnp.int32, (block, quarter), 1) < quarter // 2
    for u in range(0, rows5, block):
        lhs = jnp.concatenate(
            [half6[x, part, u : u + block, :] for x in range(4) for part in range(2)], axis=0
        )
        y = dot(lhs, b6[...])
        for tile in range(4):
            cols = slice(tile * quarter, (tile + 1) * quarter)
            re = None
            for q in range(2):
                at = q * 4 * block
                pr = y[at : at + block, cols]
                pi = y[at + block : at + 2 * block, cols]
                qr = y[at + 2 * block : at + 3 * block, cols]
                qi = y[at + 3 * block : at + 4 * block, cols]
                place = (tile + q) % 4
                c = tab5[place % 2, 0, u : u + block, :]
                s = tab5[place % 2, 1, u : u + block, :]
                if place >= 2:
                    dr = c * pr + s * qi
                    di = c * pi - s * qr
                else:
                    dr = c * pr - s * qi
                    di = c * pi + s * qr
                if q == 0:
                    re, im = dr, di
                else:
                    re, im = re + dr, im + di
            if_low = jnp.where(low_lane, re, pltpu.roll(im, quarter // 2, 1)).astype(BF16)
            if_high = jnp.where(low_lane, pltpu.roll(re, quarter // 2, 1), im).astype(BF16)
            for r in range(0, block, 16):
                band = (u + r) // 16
                out[2 * tile * 16 + band, 0] = if_low[r : r + 16, :]
                out[(2 * tile + 1) * 16 + band, 0] = if_high[r : r + 16, :]


def aggregate(patterns7, polar_up7, azimuth_up7, polar_up6, azimuth_up6):
    children, _, rows7, cols7 = patterns7.shape
    rows6, rows5 = polar_up7.shape[0], polar_up6.shape[0]
    cols6, cols5 = azimuth_up7.shape[1], azimuth_up6.shape[1]
    clusters = children // 64
    pat = patterns7.reshape(children * 2 * rows7, cols7)
    top7, bottom7 = fold_factors(rows6, rows7)
    z = theta_phase(rows5)[:, None]
    cz = np.broadcast_to(np.cos(z), (rows5, rows6)).astype(np.float32)
    sz = np.broadcast_to(np.sin(z), (rows5, rows6)).astype(np.float32)
    f0, f1 = plane_phases(rows6, cols6, cols6 // 2)
    tab6 = np.stack([np.cos(f0), np.sin(f0), np.cos(f1), np.sin(f1)]).astype(np.float32)
    g0, _ = plane_phases(rows5, cols5, cols5 // 2)
    g0 = g0.reshape(rows5, 2, cols5 // 4).transpose(1, 0, 2)
    tab5 = np.stack([np.cos(g0), np.sin(g0)], axis=1).astype(np.float32)
    full = lambda shape: pl.BlockSpec(shape, lambda g: (0,) * len(shape))
    consts = (top7, bottom7, cz, sz, tab6, tab5)
    weights = (polar_up7.T, azimuth_up7, polar_up6, azimuth_up6)
    lines = pat.shape[0] // clusters
    return pl.pallas_call(
        aggregate_body,
        grid=(clusters,),
        in_specs=[pl.BlockSpec((lines, cols7), lambda g: (g, 0))]
        + [full(a.shape) for a in weights]
        + [full(a.shape) for a in consts],
        out_specs=pl.BlockSpec((128, 1, 16, 128), lambda g: (0, g, 0, 0)),
        out_shape=jax.ShapeDtypeStruct((128, clusters, 16, 128), BF16),
        scratch_shapes=[
            pltpu.VMEM((2 * rows6, 4 * rows7), BF16),
            pltpu.VMEM((2, rows5, 2 * rows6), BF16),
            pltpu.VMEM((8, 2, rows6, cols6), F32),
            pltpu.VMEM((4, 2, 2, rows6, cols6), BF16),
            pltpu.VMEM((4, 2, rows5, cols6), BF16),
        ],
        compiler_params=pltpu.CompilerParams(vmem_limit_bytes=58 * 1024 * 1024),
        name="aggregate",
    )(pat, *weights, *[jnp.asarray(a) for a in consts])


def table_body(tr, out):
    theta = pl.program_id(0)
    entries = out.shape[0] // 16
    count = tr.shape[4]
    stack = jnp.concatenate([tr[0, 0, 0], tr[0, 1, 0], tr[1, 0, 0], tr[1, 1, 0]], axis=0)
    row = lax.broadcasted_iota(jnp.int32, (entries, count), 0)
    col = lax.broadcasted_iota(jnp.int32, (entries, count), 1)
    unit = jnp.where(row == col, 1.0, 0.0).astype(BF16)
    turned = dot_t(unit, stack)
    out[pl.ds(theta, entries, 16), :] = turned[:, :128]
    out[pl.ds(theta + 8, entries, 16), :] = turned[:, 128:]


def transfer_table(transfer):
    count, _, rows, cols = transfer.shape
    entries = (count + 1 + 7) // 8 * 8
    turned = transfer.transpose(1, 2, 3, 0).reshape(2, 2, rows // 2, cols, count)
    return pl.pallas_call(
        table_body,
        grid=(rows // 2,),
        in_specs=[pl.BlockSpec((2, 2, 1, cols, count), lambda i: (0, 0, i, 0, 0))],
        out_specs=pl.BlockSpec((entries * 16, 128), lambda i: (0, 0)),
        out_shape=jax.ShapeDtypeStruct((entries * 16, 128), F32),
        compiler_params=pltpu.CompilerParams(vmem_limit_bytes=12 * 1024 * 1024),
        name="transfer_table",
    )(turned)


def tree(terms):
    while len(terms) > 1:
        rest = terms[len(terms) // 2 * 2 :]
        terms = [terms[i] + terms[i + 1] for i in range(0, len(terms) - 1, 2)] + rest
    return terms[0]


def by_class(order, starts, slots, group, one):
    for index, count in enumerate(slot_classes(slots)):
        begin, end = starts[index], starts[index + 1]

        def some(i, carry, begin=begin, end=end, count=count):
            for k in range(group):
                one(order[jnp.minimum(begin + i * group + k, end - 1)], count)
            return carry

        lax.fori_loop(0, (end - begin + group - 1) // group, some, 0)


def slot_classes(slots):
    return tuple(range(slots // 2, slots + 1, 2))


def target_classes(sources):
    targets, slots = sources.shape
    live = jnp.sum((sources >= 0).astype(jnp.int32), axis=1)
    kind = sum((live > count).astype(jnp.int32) for count in slot_classes(slots)[:-1])
    index = jnp.arange(targets, dtype=jnp.int32)
    key = kind * targets + index
    place = jnp.sum((key[None, :] < key[:, None]).astype(jnp.int32), axis=1)
    order = jnp.sum(jnp.where(place[None, :] == index[:, None], index[None, :], 0), axis=1)
    kinds = jnp.arange(len(slot_classes(slots)) + 1, dtype=jnp.int32)
    starts = jnp.sum((kind[None, :] < kinds[:, None]).astype(jnp.int32), axis=1)
    return order, starts


def translate_targets(src, off, order, starts, tiles, table, total, out):
    targets, lanes = order.shape[0], tiles.shape[1]
    slots = src.shape[0] // targets

    def one(t, count):
        terms_r, terms_i = [], []
        for j in range(count):
            s = pl.multiple_of(src[t * slots + j], 16)
            o = pl.multiple_of(off[t * slots + j], 16)
            xr = tiles[pl.ds(s, 8), :]
            xi = tiles[pl.ds(s + 8, 8), :]
            wr = table[pl.ds(o, 8), :]
            wi = table[pl.ds(o + 8, 8), :]
            terms_r.append(wr * xr - wi * xi)
            terms_i.append(wr * xi + wi * xr)
        at = pl.multiple_of(t * 16, 16)
        total[pl.ds(at, 8), :] = tree(terms_r)
        total[pl.ds(at + 8, 8), :] = tree(terms_i)

    by_class(order, starts, slots, 4, one)
    unit = jnp.where(
        lax.broadcasted_iota(jnp.int32, (lanes, lanes), 0)
        == lax.broadcasted_iota(jnp.int32, (lanes, lanes), 1),
        1.0,
        0.0,
    ).astype(BF16)
    for row in range(16):
        turned = dot_t(unit, total[pl.ds(row, targets, 16), :].astype(BF16)).astype(BF16)
        out[row // 8, row % 8] = turned[: lanes // 2]
        out[row // 8, row % 8 + 8] = turned[lanes // 2 :]


def first_targets_body(src, off, order, starts, level, table_from, out, tiles, table, total, sem):
    clusters, rows, lanes = level.shape
    low = lax.broadcasted_iota(jnp.int32, (8, lanes), 1) < lanes // 2
    fetch = pltpu.make_async_copy(table_from, table, sem)
    fetch.start()

    def widen(t, carry):
        x = level[t].astype(F32)
        upper, lower = x[:8], x[8:]
        at = pl.multiple_of(t * 16, 16)
        tiles[pl.ds(at, 8), :] = jnp.where(low, upper, pltpu.roll(lower, lanes // 2, 1))
        tiles[pl.ds(at + 8, 8), :] = jnp.where(low, pltpu.roll(upper, lanes // 2, 1), lower)
        return carry

    lax.fori_loop(0, clusters, widen, 0, unroll=16)
    fetch.wait()
    translate_targets(src, off, order, starts, tiles, table, total, out)


def last_targets_body(
    src, off, order, starts, tiles, table, before, out, total, turned, sem_before, sem_after
):
    targets = order.shape[0]
    pass_on = pltpu.make_async_copy(before, out.at[:, :, :, pl.ds(0, targets)], sem_before)
    pass_on.start()
    translate_targets(src, off, order, starts, tiles, table, total, turned)
    finish = pltpu.make_async_copy(turned, out.at[:, :, :, pl.ds(targets, targets)], sem_after)
    finish.start()
    finish.wait()
    pass_on.wait()


SMEM_SPEC = pl.BlockSpec(memory_space=pltpu.SMEM)
VMEM_SPEC = pl.BlockSpec(memory_space=pltpu.VMEM)
ANY_SPEC = pl.BlockSpec(memory_space=pl.ANY)


def translate_first(level, table, lists):
    clusters, rows, lanes = level.shape
    targets = lists[2].shape[0]
    table = pltpu.with_memory_space_constraint(table, pltpu.HBM)
    return pl.pallas_call(
        first_targets_body,
        in_specs=[SMEM_SPEC] * 4 + [VMEM_SPEC, pl.BlockSpec(memory_space=pltpu.HBM)],
        out_specs=(VMEM_SPEC,) * 3,
        out_shape=(
            jax.ShapeDtypeStruct((2, rows, lanes // 2, targets), BF16),
            jax.ShapeDtypeStruct((clusters * 16, lanes), F32),
            jax.ShapeDtypeStruct(table.shape, F32),
        ),
        scratch_shapes=[pltpu.VMEM((targets * 16, lanes), F32), pltpu.SemaphoreType.DMA],
        compiler_params=pltpu.CompilerParams(vmem_limit_bytes=20 * 1024 * 1024),
        name="translate_first",
    )(*lists, level, table)


def translate_last(tiles, table, before, lists):
    parts, rows, half, targets = before.shape
    turned = pl.pallas_call(
        last_targets_body,
        in_specs=[SMEM_SPEC] * 4 + [VMEM_SPEC] * 3,
        out_specs=ANY_SPEC,
        out_shape=jax.ShapeDtypeStruct((parts, rows, half, 2 * targets), BF16),
        scratch_shapes=[
            pltpu.VMEM((targets * 16, tiles.shape[1]), F32),
            pltpu.VMEM(before.shape, BF16),
            pltpu.SemaphoreType.DMA,
            pltpu.SemaphoreType.DMA,
        ],
        compiler_params=pltpu.CompilerParams(vmem_limit_bytes=20 * 1024 * 1024),
        name="translate_last",
    )(*lists, tiles, table, before)
    return turned.transpose(3, 0, 1, 2)


def edge_picks():
    pick = np.zeros((96, 256), np.float32)
    for side in range(2):
        for n in range(48):
            parent, child, j = n // 24, n % 24 // 3, n % 3
            pick[side * 48 + n, parent * 128 + child * 16 + (13 if side == 0 else 0) + j] = 1.0
    return pick


def edge_columns_body(level, right, left):
    lane = lax.broadcasted_iota(jnp.int32, (1024, 256), 0)
    col = lax.broadcasted_iota(jnp.int32, (1024, 256), 1)
    side = col >> 7
    place = lane >> 7
    part = (lane >> 6) & 1
    j = col & 3
    hit = (
        (((col & 127) >> 4) == place)
        & (((col >> 3) & 1) == side)
        & (((col >> 2) & 1) == part)
        & (j < 3)
        & ((lane & 63) == jnp.where(side == 0, 61 + j, j))
    )
    spread = jnp.where(hit, 1.0, 0.0).astype(BF16)
    for g in range(8):
        lhs = jnp.concatenate([level[8 * g + i] for i in range(8)], axis=1)
        both = dot(lhs, spread).astype(BF16)
        right[g] = both[:, :128]
        left[g] = both[:, 128:]


def edge_columns(level):
    return pl.pallas_call(
        edge_columns_body,
        out_shape=(jax.ShapeDtypeStruct((8, 128, 128), BF16),) * 2,
        compiler_params=pltpu.CompilerParams(vmem_limit_bytes=10 * 1024 * 1024),
        name="edge_columns",
    )(level)


def edge_rows_body(level, from_left, from_right, pick, sides, last, first):
    for g in range(sides.shape[0]):
        sides[g] = from_left[g] + from_right[g]
    own = level.shape[0] // 2
    for i in range(last.shape[0]):
        source, at = (level, 2 * i) if i < own else (sides, 2 * (i - own))
        both = dot(pick[...], jnp.concatenate([source[at], source[at + 1]], axis=0)).astype(BF16)
        last[i] = both[:48]
        first[i] = both[48:]


def edge_rows(level, from_left, from_right):
    pairs = (level.shape[0] + from_left.shape[0]) // 2
    return pl.pallas_call(
        edge_rows_body,
        out_shape=(jax.ShapeDtypeStruct(from_left.shape, BF16),)
        + (jax.ShapeDtypeStruct((pairs, 48, 128), BF16),) * 2,
        compiler_params=pltpu.CompilerParams(vmem_limit_bytes=8 * 1024 * 1024),
        name="edge_rows",
    )(level, from_left, from_right, jnp.asarray(edge_picks(), BF16))


def stencil_maps():
    ext = np.zeros((1, 224), np.int32)
    factor = np.zeros((2, 8, 224), np.float32)
    sign = np.zeros((4, 8))
    for q, (a, b) in enumerate(PAIRS):
        for h in range(2):
            sign[2 * q, a + 4 * h] = sign[2 * q, b + 4 * h] = 1.0
            sign[2 * q + 1, a + 4 * h] = 1.0
            sign[2 * q + 1, b + 4 * h] = -1.0
    for col in range(224):
        if col < 128:
            owner, child, ext[0, col] = (0, 1), col // 16, col % 16 + 3
        else:
            n = (col - 128) % 48
            owner, child = (n // 24,), n % 24 // 3
            ext[0, col] = n % 3 + (0 if col < 176 else 19)
        for parity in owner:
            for x in range(4):
                factor[parity, 2 * x, col] = sign[x, child]
                factor[parity, 2 * x + 1, col] = sign[x, child] * (1.0 if child >= 4 else -1.0)
    return ext, factor


def stencils_body(tap_u, weight_u, trig, tap_v, weight_v, ext, factor, polar, azimuth):
    rows = tap_u.shape[0]
    base = jnp.zeros((rows, ext.shape[1]), F32)
    for k in range(4):
        base = base + jnp.where(tap_u[:, k : k + 1] == ext[...], weight_u[:, k : k + 1], 0.0)
    for parity in range(2):
        for kind in range(8):
            turned = base * trig[:, kind % 2 : kind % 2 + 1]
            polar[parity, kind * rows : (kind + 1) * rows, :] = (
                turned * factor[parity, kind : kind + 1, :]
            ).astype(BF16)
    i = lax.broadcasted_iota(jnp.int32, (128, 128), 0)

    def fill(at, matrix, part, index):
        first = part == 0
        azimuth[index, at : at + 128, :128] = jnp.where(first, matrix, 0.0).astype(BF16)
        azimuth[index, at : at + 128, 128:] = jnp.where(first, 0.0, matrix).astype(BF16)

    def matrix_at(q):
        total = jnp.zeros((128, 128), F32)
        for k in range(4):
            total = total + jnp.where(tap_v[k : k + 1, :] == q, weight_v[k : k + 1, :], 0.0)
        return total

    own = matrix_at((i & 63) + 3)
    j = i & 3
    halo = jnp.where(j < 3, matrix_at(j + 67 * ((i >> 3) & 1)), 0.0)
    for index in range(8):
        fill(0, own, i >> 6, index)
        fill(128, jnp.where((i >> 4) == index, halo, 0.0), (i >> 2) & 1, index)


def stencils(tap_u, weight_u, trig, tap_v, weight_v):
    ext, factor = stencil_maps()
    rows = tap_u.shape[0]
    return pl.pallas_call(
        stencils_body,
        out_shape=(
            jax.ShapeDtypeStruct((2, 8 * rows, 224), BF16),
            jax.ShapeDtypeStruct((8, 256, 256), BF16),
        ),
        compiler_params=pltpu.CompilerParams(vmem_limit_bytes=8 * 1024 * 1024),
        name="stencils",
    )(tap_u, weight_u, trig, tap_v, weight_v, jnp.asarray(ext), jnp.asarray(factor))


def theta_stage(level, low, high, at, polar, half, swap):
    for i in range(level.shape[0] // 2):
        for parity in range(2):
            rhs = jnp.concatenate([level[2 * i + parity], low[at + i], high[at + i]], axis=0)
            y = dot(polar[parity], rhs)
            for x in range(4):
                c, s = y[64 * x : 64 * x + 32], y[64 * x + 32 : 64 * x + 64]
                half[2 * i + parity, 32 * x : 32 * x + 32] = (c + swap(s)).astype(BF16)


def top_body(
    src, off, order, starts, level, sides, low, high, polar, azimuth, tab, transfer, out,
    table, half, side_half, level4, sem,
):
    count = transfer.shape[0]
    fetch = pltpu.make_async_copy(transfer, table.at[pl.ds(0, count)], sem)
    fetch.start()
    table[count] = jnp.zeros(table.shape[1:], BF16)
    lane = lax.broadcasted_iota(jnp.int32, (32, 128), 1)
    wide = jnp.where(lane < 64, -1.0, 1.0)
    real = (lane & 4) == 0

    def swap_wide(s):
        return pltpu.roll(s, 64, 1) * wide

    def swap_near(s):
        return jnp.where(real, -pltpu.roll(s, 124, 1), pltpu.roll(s, 4, 1))

    theta_stage(level, low, high, 0, polar, half, swap_wide)
    theta_stage(sides, low, high, level.shape[0] // 2, polar, side_half, swap_near)

    def phi_stage(place, carry):
        rows = []
        for g in range(8):
            for x in range(4):
                a = slice(32 * x, 32 * x + 32)
                rows.append(jnp.concatenate([half[8 * g + place, a], side_half[g, a]], axis=1))
        y = dot(jnp.concatenate(rows, axis=0), azimuth[place])
        for g in range(8):
            re = im = None
            for q in range(2):
                at = 128 * g + 64 * q
                pr = y[at : at + 32, :128]
                pi = y[at : at + 32, 128:]
                qr = y[at + 32 : at + 64, :128]
                qi = y[at + 32 : at + 64, 128:]
                c = tab[2 * q]
                s = tab[2 * q + 1]
                dr = c * pr - s * qi
                di = c * pi + s * qr
                re, im = (dr, di) if q == 0 else (re + dr, im + di)
            at = pl.multiple_of((8 * g + place) * 64, 64)
            level4[pl.ds(at, 32), :] = re
            level4[pl.ds(at + 32, 32), :] = im
        return carry

    lax.fori_loop(0, 8, phi_stage, 0)
    fetch.wait()
    targets = out.shape[0]
    slots = src.shape[0] // targets

    def one(t, count):
        re = [jnp.zeros((8, 128), F32)] * 4
        im = [jnp.zeros((8, 128), F32)] * 4
        for j in range(count):
            at = pl.multiple_of(src[t * slots + j], 64)
            w = table.at[off[t * slots + j]]
            for r in range(4):
                xr = level4[pl.ds(at + 8 * r, 8), :]
                xi = level4[pl.ds(at + 32 + 8 * r, 8), :]
                wr = w[0, 8 * r : 8 * r + 8].astype(F32)
                wi = w[1, 8 * r : 8 * r + 8].astype(F32)
                re[r] = re[r] + (wr * xr - wi * xi)
                im[r] = im[r] + (wr * xi + wi * xr)
        for r in range(4):
            out[t, 0, 8 * r : 8 * r + 8] = re[r].astype(BF16)
            out[t, 1, 8 * r : 8 * r + 8] = im[r].astype(BF16)

    by_class(order, starts, slots, 1, one)


def top_level(level, sides, low, high, polar, azimuth, tab, transfer, lists):
    count, _, rows, cols = transfer.shape
    parents = level.shape[0]
    lines = (polar.shape[1] // 2, level.shape[2])
    return pl.pallas_call(
        top_body,
        in_specs=[SMEM_SPEC] * 4 + [VMEM_SPEC] * 7 + [ANY_SPEC],
        out_specs=VMEM_SPEC,
        out_shape=jax.ShapeDtypeStruct((parents, 2, rows, cols), BF16),
        scratch_shapes=[
            pltpu.VMEM((count + 1, 2, rows, cols), BF16),
            pltpu.VMEM((parents,) + lines, BF16),
            pltpu.VMEM((sides.shape[0],) + lines, BF16),
            pltpu.VMEM((parents * 2 * rows, cols), F32),
            pltpu.SemaphoreType.DMA,
        ],
        compiler_params=pltpu.CompilerParams(vmem_limit_bytes=30 * 1024 * 1024),
        name="top_level",
    )(*lists, level, sides, low, high, polar, azimuth, tab, transfer)


def flat_lists(sources, offsets, dead, source_rows, factor_rows):
    src = jnp.maximum(sources, 0) * source_rows
    off = jnp.where(offsets < 0, dead, offsets) * factor_rows
    return (src.reshape(-1), off.reshape(-1)) + target_classes(sources)


def shards(
    patterns7,
    polar_up7,
    azimuth_up7,
    polar_up6,
    azimuth_up6,
    polar_first,
    polar_weights,
    azimuth_first,
    azimuth_weights,
    transfer5,
    sources5,
    offsets5,
    transfer4,
    sources4,
    offsets4,
):
    bands = lax.axis_size("ang")
    blocks = lax.axis_size("clu")
    band = lax.axis_index("ang")
    block = lax.axis_index("clu")

    send = aggregate(patterns7, polar_up7, azimuth_up7, polar_up6, azimuth_up6)
    arrived = lax.all_to_all(send, ("clu", "ang"), split_axis=0, concat_axis=0, tiled=True)

    count5 = transfer5.shape[0]
    count4 = transfer4.shape[0]
    table5 = transfer_table(transfer5)
    half5 = sources5.shape[0] // 2
    lists5 = (
        flat_lists(sources5[:half5], offsets5[:half5], count5, 16, 16),
        flat_lists(sources5[half5:], offsets5[half5:], count5, 16, 16),
    )
    lists4 = flat_lists(sources4, offsets4, count4, 64, 1)
    rows4 = polar_first.shape[0]
    cols4 = azimuth_first.shape[0]
    band_rows = rows4 // bands
    block_cols = cols4 // blocks
    taps = jnp.arange(4, dtype=jnp.int32)
    tap_u = lax.dynamic_slice_in_dim(polar_first, band * band_rows, band_rows, 0)
    tap_u = (tap_u - band * (band_rows // 2) + 3)[:, None] + taps[None, :]
    weight_u = lax.dynamic_slice_in_dim(polar_weights, band * band_rows, band_rows, 0).astype(F32)
    tap_v = lax.dynamic_slice_in_dim(azimuth_first, block * block_cols, block_cols, 0)
    tap_v = (tap_v[None, :] + taps[:, None] - block * (block_cols // 2) + 3) % (cols4 // 2)
    weight_v = lax.dynamic_slice_in_dim(azimuth_weights, block * block_cols, block_cols, 0)
    weight_v = weight_v.T.astype(F32)
    theta = (jnp.arange(band_rows, dtype=jnp.int32) + band * band_rows).astype(F32)
    theta = (theta + 0.5) * (math.pi / rows4)
    phi = (jnp.arange(block_cols, dtype=jnp.int32) + block * block_cols).astype(F32)
    phi = phi * (2.0 * math.pi / cols4)
    scale = rows4 / 8.0
    lift = scale * jnp.cos(theta)
    trig = jnp.stack([jnp.cos(lift), jnp.sin(lift)], axis=1)
    x = jnp.sin(theta)[:, None] * jnp.cos(phi)[None, :]
    y = jnp.sin(theta)[:, None] * jnp.sin(phi)[None, :]
    f0 = scale * (x + y)
    f1 = scale * (x - y)
    tab = jnp.stack([jnp.cos(f0), jnp.sin(f0), jnp.cos(f1), jnp.sin(f1)])
    polar, azimuth = stencils(tap_u, weight_u, trig, tap_v, weight_v)
    arrived, table5, lists5, lists4, polar, azimuth, tab = lax.optimization_barrier(
        (arrived, table5, lists5, lists4, polar, azimuth, tab)
    )

    level = arrived.reshape(64, 128, 128)
    right, left = edge_columns(level)
    around = lambda step: [(i, (i + step) % blocks) for i in range(blocks)]
    across = lambda step: [(i, i + step) for i in range(bands) if 0 <= i + step < bands]
    from_left = lax.ppermute(right, "clu", around(1))
    from_right = lax.ppermute(left, "clu", around(-1))
    before, tiles, table5 = translate_first(arrived.reshape(512, 16, 128), table5, lists5[0])
    from_left, from_right, tiles = lax.optimization_barrier((from_left, from_right, tiles))
    sides, last, first = edge_rows(level, from_left, from_right)
    last, first, tiles = lax.optimization_barrier((last, first, tiles))
    low = lax.ppermute(last, "ang", across(1))
    high = lax.ppermute(first, "ang", across(-1))
    translated5 = translate_last(tiles, table5, before, lists5[1])
    translated4 = top_level(
        level, sides, low, high, polar, azimuth, tab, transfer4, lists4
    )
    return (translated5, translated4)


def solution(mesh):
    in_specs = (
        P(("clu", "ang"), None, None, None),
        P(),
        P(),
        P(),
        P(),
        P(),
        P(),
        P(),
        P(),
        P(None, None, "ang", "clu"),
        P(),
        P(),
        P(None, None, "ang", "clu"),
        P(),
        P(),
    )
    out_specs = (P(None, None, "ang", "clu"), P(None, None, "ang", "clu"))
    return jax.shard_map(shards, mesh=mesh, in_specs=in_specs, out_specs=out_specs, check_vma=False)
```

```python
import math

import jax
import jax.numpy as jnp
import numpy as np
from jax import lax
from jax.experimental import pallas as pl
from jax.experimental.pallas import tpu as pltpu
from jax.sharding import PartitionSpec as P

F32 = jnp.float32
BF16 = jnp.bfloat16
TOGETHER = 2
BLOCK5 = 128


PAIRS = ((3, 0), (1, 2))


def theta_phase(rows):
    return rows / 8.0 * np.cos(np.pi * (np.arange(rows) + 0.5) / rows)


def plane_phases(rows, cols, count):
    theta = np.pi * (np.arange(rows) + 0.5) / rows
    phi = 2.0 * np.pi * np.arange(count) / cols
    x = np.sin(theta)[:, None] * np.cos(phi)[None, :]
    y = np.sin(theta)[:, None] * np.sin(phi)[None, :]
    return rows / 8.0 * (x + y), rows / 8.0 * (x - y)


def fold_factors(rows, inner):
    phase = theta_phase(rows)[:, None]
    cosine = np.broadcast_to(np.cos(phase), (rows, inner))
    sine = np.broadcast_to(np.sin(phase), (rows, inner))
    top = np.concatenate([cosine, sine, cosine, -sine], axis=1)
    bottom = np.concatenate([-sine, cosine, sine, cosine], axis=1)
    return top.astype(np.float32), bottom.astype(np.float32)


def dot(a, b):
    return jnp.dot(a, b, preferred_element_type=F32)


def dot_t(a, b):
    return lax.dot_general(a, b, (((1,), (1,)), ((), ())), preferred_element_type=F32)


def aggregate_body(
    pat, a7, b7, a6, b6, top7, bottom7, cz, sz, tab6, tab5, out, m7, m6, level6, mixed, half6
):
    rows7, rows6, rows5 = a7.shape[0], a7.shape[1], a6.shape[0]
    cols6, cols5 = b7.shape[1], b6.shape[1]

    @pl.when(pl.program_id(0) == 0)
    def _():
        src = lax.broadcasted_iota(jnp.int32, (rows7, 4 * rows7), 0)
        dst = lax.broadcasted_iota(jnp.int32, (rows7, 4 * rows7), 1)
        spread = jnp.where((dst & (rows7 - 1)) == src, 1.0, 0.0).astype(BF16)
        wide = lax.dot_general(
            a7[...], spread, (((0,), (0,)), ((), ())), preferred_element_type=F32
        )
        m7[0:rows6, :] = (wide * top7[...]).astype(BF16)
        m7[rows6 : 2 * rows6, :] = (wide * bottom7[...]).astype(BF16)
        base = a6[...].astype(F32)
        c = base * cz[...]
        s = base * sz[...]
        m6[0, :, 0:rows6] = c.astype(BF16)
        m6[0, :, rows6 : 2 * rows6] = (-s).astype(BF16)
        m6[1, :, 0:rows6] = c.astype(BF16)
        m6[1, :, rows6 : 2 * rows6] = s.astype(BF16)

    step = 2 * rows7
    for first in range(0, 8, TOGETHER):
        stacks = []
        for o6 in range(first, first + TOGETHER):
            base = o6 * 8 * step
            for k in range(4):
                low = pat[base + k * step : base + (k + 1) * step, :]
                high = pat[base + (k + 4) * step : base + (k + 5) * step, :]
                stacks.append(jnp.concatenate([low, high], axis=0))
        lanes = stacks[0].shape[1]
        h = dot(m7[...], jnp.concatenate(stacks, axis=1))
        rows = []
        for n in range(TOGETHER):
            for a, b in PAIRS:
                ya = h[:, (4 * n + a) * lanes : (4 * n + a + 1) * lanes]
                yb = h[:, (4 * n + b) * lanes : (4 * n + b + 1) * lanes]
                rows.append((ya + yb).astype(BF16))
                rows.append((ya - yb).astype(BF16))
        everything = dot(jnp.concatenate(rows, axis=0), b7[...])
        for n in range(TOGETHER):
            y = everything[n * 8 * rows6 : (n + 1) * 8 * rows6]
            for half in range(2):
                cols = slice(half * (cols6 // 2), (half + 1) * (cols6 // 2))
                re = None
                for q in range(2):
                    at = q * 4 * rows6
                    pr = y[at : at + rows6, cols]
                    pi = y[at + rows6 : at + 2 * rows6, cols]
                    qr = y[at + 2 * rows6 : at + 3 * rows6, cols]
                    qi = y[at + 3 * rows6 : at + 4 * rows6, cols]
                    c = tab6[2 * q]
                    s = tab6[2 * q + 1]
                    if half == 1:
                        dr = c * pr + s * qi
                        di = c * pi - s * qr
                    else:
                        dr = c * pr - s * qi
                        di = c * pi + s * qr
                    re, im = (dr, di) if re is None else (re + dr, im + di)
                level6[first + n, 0, :, cols] = re
                level6[first + n, 1, :, cols] = im

    for part in range(2):
        for r in range(0, rows6, 16):
            x = [level6[o, part, r : r + 16, :] for o in range(8)]
            for t in range(2):
                z = [x[k + 4] + x[k] if t == 0 else x[k + 4] - x[k] for k in range(4)]
                for q, (a, b) in enumerate(PAIRS):
                    mixed[2 * q, t, part, r : r + 16, :] = (z[a] + z[b]).astype(BF16)
                    mixed[2 * q + 1, t, part, r : r + 16, :] = (z[a] - z[b]).astype(BF16)

    for x in range(4):
        for part in range(2):
            rhs = jnp.concatenate([mixed[x, 0, part], mixed[x, 1, 1 - part]], axis=0)
            half6[x, part] = dot(m6[part], rhs).astype(BF16)

    block = BLOCK5
    quarter = cols5 // 4
    low_lane = lax.broadcasted_iota(jnp.int32, (block, quarter), 1) < quarter // 2
    for u in range(0, rows5, block):
        lhs = jnp.concatenate(
            [half6[x, part, u : u + block, :] for x in range(4) for part in range(2)], axis=0
        )
        y = dot(lhs, b6[...])
        for tile in range(4):
            cols = slice(tile * quarter, (tile + 1) * quarter)
            re = None
            for q in range(2):
                at = q * 4 * block
                pr = y[at : at + block, cols]
                pi = y[at + block : at + 2 * block, cols]
                qr = y[at + 2 * block : at + 3 * block, cols]
                qi = y[at + 3 * block : at + 4 * block, cols]
                place = (tile + q) % 4
                c = tab5[place % 2, 0, u : u + block, :]
                s = tab5[place % 2, 1, u : u + block, :]
                if place >= 2:
                    dr = c * pr + s * qi
                    di = c * pi - s * qr
                else:
                    dr = c * pr - s * qi
                    di = c * pi + s * qr
                if q == 0:
                    re, im = dr, di
                else:
                    re, im = re + dr, im + di
            if_low = jnp.where(low_lane, re, pltpu.roll(im, quarter // 2, 1)).astype(BF16)
            if_high = jnp.where(low_lane, pltpu.roll(re, quarter // 2, 1), im).astype(BF16)
            for r in range(0, block, 16):
                band = (u + r) // 16
                out[2 * tile * 16 + band, 0] = if_low[r : r + 16, :]
                out[(2 * tile + 1) * 16 + band, 0] = if_high[r : r + 16, :]


def aggregate(patterns7, polar_up7, azimuth_up7, polar_up6, azimuth_up6):
    children, _, rows7, cols7 = patterns7.shape
    rows6, rows5 = polar_up7.shape[0], polar_up6.shape[0]
    cols6, cols5 = azimuth_up7.shape[1], azimuth_up6.shape[1]
    clusters = children // 64
    pat = patterns7.reshape(children * 2 * rows7, cols7)
    top7, bottom7 = fold_factors(rows6, rows7)
    z = theta_phase(rows5)[:, None]
    cz = np.broadcast_to(np.cos(z), (rows5, rows6)).astype(np.float32)
    sz = np.broadcast_to(np.sin(z), (rows5, rows6)).astype(np.float32)
    f0, f1 = plane_phases(rows6, cols6, cols6 // 2)
    tab6 = np.stack([np.cos(f0), np.sin(f0), np.cos(f1), np.sin(f1)]).astype(np.float32)
    g0, _ = plane_phases(rows5, cols5, cols5 // 2)
    g0 = g0.reshape(rows5, 2, cols5 // 4).transpose(1, 0, 2)
    tab5 = np.stack([np.cos(g0), np.sin(g0)], axis=1).astype(np.float32)
    full = lambda shape: pl.BlockSpec(shape, lambda g: (0,) * len(shape))
    consts = (top7, bottom7, cz, sz, tab6, tab5)
    weights = (polar_up7.T, azimuth_up7, polar_up6, azimuth_up6)
    lines = pat.shape[0] // clusters
    return pl.pallas_call(
        aggregate_body,
        grid=(clusters,),
        in_specs=[pl.BlockSpec((lines, cols7), lambda g: (g, 0))]
        + [full(a.shape) for a in weights]
        + [full(a.shape) for a in consts],
        out_specs=pl.BlockSpec((128, 1, 16, 128), lambda g: (0, g, 0, 0)),
        out_shape=jax.ShapeDtypeStruct((128, clusters, 16, 128), BF16),
        scratch_shapes=[
            pltpu.VMEM((2 * rows6, 4 * rows7), BF16),
            pltpu.VMEM((2, rows5, 2 * rows6), BF16),
            pltpu.VMEM((8, 2, rows6, cols6), F32),
            pltpu.VMEM((4, 2, 2, rows6, cols6), BF16),
            pltpu.VMEM((4, 2, rows5, cols6), BF16),
        ],
        compiler_params=pltpu.CompilerParams(vmem_limit_bytes=58 * 1024 * 1024),
        name="aggregate",
    )(pat, *weights, *[jnp.asarray(a) for a in consts])


def table_body(tr, out):
    theta = pl.program_id(0)
    entries = out.shape[0] // 16
    count = tr.shape[4]
    stack = jnp.concatenate([tr[0, 0, 0], tr[0, 1, 0], tr[1, 0, 0], tr[1, 1, 0]], axis=0)
    row = lax.broadcasted_iota(jnp.int32, (entries, count), 0)
    col = lax.broadcasted_iota(jnp.int32, (entries, count), 1)
    unit = jnp.where(row == col, 1.0, 0.0).astype(BF16)
    turned = dot_t(unit, stack)
    out[pl.ds(theta, entries, 16), :] = turned[:, :128]
    out[pl.ds(theta + 8, entries, 16), :] = turned[:, 128:]


def transfer_table(transfer):
    count, _, rows, cols = transfer.shape
    entries = (count + 1 + 7) // 8 * 8
    turned = transfer.transpose(1, 2, 3, 0).reshape(2, 2, rows // 2, cols, count)
    return pl.pallas_call(
        table_body,
        grid=(rows // 2,),
        in_specs=[pl.BlockSpec((2, 2, 1, cols, count), lambda i: (0, 0, i, 0, 0))],
        out_specs=pl.BlockSpec((entries * 16, 128), lambda i: (0, 0)),
        out_shape=jax.ShapeDtypeStruct((entries * 16, 128), F32),
        compiler_params=pltpu.CompilerParams(vmem_limit_bytes=12 * 1024 * 1024),
        name="transfer_table",
    )(turned)


def tree(terms):
    while len(terms) > 1:
        rest = terms[len(terms) // 2 * 2 :]
        terms = [terms[i] + terms[i + 1] for i in range(0, len(terms) - 1, 2)] + rest
    return terms[0]


def by_class(order, starts, slots, group, one):
    for index, count in enumerate(slot_classes(slots)):
        begin, end = starts[index], starts[index + 1]

        def some(i, carry, begin=begin, end=end, count=count):
            for k in range(group):
                one(order[jnp.minimum(begin + i * group + k, end - 1)], count)
            return carry

        lax.fori_loop(0, (end - begin + group - 1) // group, some, 0)


def slot_classes(slots):
    return tuple(range(slots // 2, slots + 1, 2))


def target_classes(sources):
    targets, slots = sources.shape
    live = jnp.sum((sources >= 0).astype(jnp.int32), axis=1)
    kind = sum((live > count).astype(jnp.int32) for count in slot_classes(slots)[:-1])
    index = jnp.arange(targets, dtype=jnp.int32)
    key = kind * targets + index
    place = jnp.sum((key[None, :] < key[:, None]).astype(jnp.int32), axis=1)
    order = jnp.sum(jnp.where(place[None, :] == index[:, None], index[None, :], 0), axis=1)
    kinds = jnp.arange(len(slot_classes(slots)) + 1, dtype=jnp.int32)
    starts = jnp.sum((kind[None, :] < kinds[:, None]).astype(jnp.int32), axis=1)
    return order, starts


def translate_targets(src, off, order, starts, tiles, table, total, out):
    targets, lanes = order.shape[0], tiles.shape[1]
    slots = src.shape[0] // targets

    def one(t, count):
        terms_r, terms_i = [], []
        for j in range(count):
            s = pl.multiple_of(src[t * slots + j], 16)
            o = pl.multiple_of(off[t * slots + j], 16)
            xr = tiles[pl.ds(s, 8), :]
            xi = tiles[pl.ds(s + 8, 8), :]
            wr = table[pl.ds(o, 8), :]
            wi = table[pl.ds(o + 8, 8), :]
            terms_r.append(wr * xr - wi * xi)
            terms_i.append(wr * xi + wi * xr)
        at = pl.multiple_of(t * 16, 16)
        total[pl.ds(at, 8), :] = tree(terms_r)
        total[pl.ds(at + 8, 8), :] = tree(terms_i)

    by_class(order, starts, slots, 4, one)
    unit = jnp.where(
        lax.broadcasted_iota(jnp.int32, (lanes, lanes), 0)
        == lax.broadcasted_iota(jnp.int32, (lanes, lanes), 1),
        1.0,
        0.0,
    ).astype(BF16)
    for row in range(16):
        turned = dot_t(unit, total[pl.ds(row, targets, 16), :].astype(BF16)).astype(BF16)
        out[row // 8, row % 8] = turned[: lanes // 2]
        out[row // 8, row % 8 + 8] = turned[lanes // 2 :]


def first_targets_body(src, off, order, starts, level, table_from, out, tiles, table, total, sem):
    clusters, rows, lanes = level.shape
    low = lax.broadcasted_iota(jnp.int32, (8, lanes), 1) < lanes // 2
    fetch = pltpu.make_async_copy(table_from, table, sem)
    fetch.start()

    def widen(t, carry):
        x = level[t].astype(F32)
        upper, lower = x[:8], x[8:]
        at = pl.multiple_of(t * 16, 16)
        tiles[pl.ds(at, 8), :] = jnp.where(low, upper, pltpu.roll(lower, lanes // 2, 1))
        tiles[pl.ds(at + 8, 8), :] = jnp.where(low, pltpu.roll(upper, lanes // 2, 1), lower)
        return carry

    lax.fori_loop(0, clusters, widen, 0, unroll=16)
    fetch.wait()
    translate_targets(src, off, order, starts, tiles, table, total, out)


def last_targets_body(
    src, off, order, starts, tiles, table, before, out, total, turned, sem_before, sem_after
):
    targets = order.shape[0]
    pass_on = pltpu.make_async_copy(before, out.at[:, :, :, pl.ds(0, targets)], sem_before)
    pass_on.start()
    translate_targets(src, off, order, starts, tiles, table, total, turned)
    finish = pltpu.make_async_copy(turned, out.at[:, :, :, pl.ds(targets, targets)], sem_after)
    finish.start()
    finish.wait()
    pass_on.wait()


SMEM_SPEC = pl.BlockSpec(memory_space=pltpu.SMEM)
VMEM_SPEC = pl.BlockSpec(memory_space=pltpu.VMEM)
ANY_SPEC = pl.BlockSpec(memory_space=pl.ANY)


def translate_first(level, table, lists):
    clusters, rows, lanes = level.shape
    targets = lists[2].shape[0]
    table = pltpu.with_memory_space_constraint(table, pltpu.HBM)
    lists = tuple(pltpu.with_memory_space_constraint(a, pltpu.HBM) for a in lists)
    return pl.pallas_call(
        first_targets_body,
        in_specs=[SMEM_SPEC] * 4 + [VMEM_SPEC, pl.BlockSpec(memory_space=pltpu.HBM)],
        out_specs=(VMEM_SPEC,) * 3,
        out_shape=(
            jax.ShapeDtypeStruct((2, rows, lanes // 2, targets), BF16),
            jax.ShapeDtypeStruct((clusters * 16, lanes), F32),
            jax.ShapeDtypeStruct(table.shape, F32),
        ),
        scratch_shapes=[pltpu.VMEM((targets * 16, lanes), F32), pltpu.SemaphoreType.DMA],
        compiler_params=pltpu.CompilerParams(vmem_limit_bytes=20 * 1024 * 1024),
        name="translate_first",
    )(*lists, level, table)


def translate_last(tiles, table, before, lists):
    parts, rows, half, targets = before.shape
    turned = pl.pallas_call(
        last_targets_body,
        in_specs=[SMEM_SPEC] * 4 + [VMEM_SPEC] * 3,
        out_specs=ANY_SPEC,
        out_shape=jax.ShapeDtypeStruct((parts, rows, half, 2 * targets), BF16),
        scratch_shapes=[
            pltpu.VMEM((targets * 16, tiles.shape[1]), F32),
            pltpu.VMEM(before.shape, BF16),
            pltpu.SemaphoreType.DMA,
            pltpu.SemaphoreType.DMA,
        ],
        compiler_params=pltpu.CompilerParams(vmem_limit_bytes=20 * 1024 * 1024),
        name="translate_last",
    )(*lists, tiles, table, before)
    return turned.transpose(3, 0, 1, 2)


def edge_picks():
    pick = np.zeros((96, 256), np.float32)
    for side in range(2):
        for n in range(48):
            parent, child, j = n // 24, n % 24 // 3, n % 3
            pick[side * 48 + n, parent * 128 + child * 16 + (13 if side == 0 else 0) + j] = 1.0
    return pick


def edge_columns_body(level, right, left):
    lane = lax.broadcasted_iota(jnp.int32, (1024, 256), 0)
    col = lax.broadcasted_iota(jnp.int32, (1024, 256), 1)
    side = col >> 7
    place = lane >> 7
    part = (lane >> 6) & 1
    j = col & 3
    hit = (
        (((col & 127) >> 4) == place)
        & (((col >> 3) & 1) == side)
        & (((col >> 2) & 1) == part)
        & (j < 3)
        & ((lane & 63) == jnp.where(side == 0, 61 + j, j))
    )
    spread = jnp.where(hit, 1.0, 0.0).astype(BF16)
    for g in range(8):
        lhs = jnp.concatenate([level[8 * g + i] for i in range(8)], axis=1)
        both = dot(lhs, spread).astype(BF16)
        right[g] = both[:, :128]
        left[g] = both[:, 128:]


def edge_columns(level):
    return pl.pallas_call(
        edge_columns_body,
        out_shape=(jax.ShapeDtypeStruct((8, 128, 128), BF16),) * 2,
        compiler_params=pltpu.CompilerParams(vmem_limit_bytes=10 * 1024 * 1024),
        name="edge_columns",
    )(level)


def edge_rows_body(level, from_left, from_right, pick, sides, last, first):
    for g in range(sides.shape[0]):
        sides[g] = from_left[g] + from_right[g]
    own = level.shape[0] // 2
    for i in range(last.shape[0]):
        source, at = (level, 2 * i) if i < own else (sides, 2 * (i - own))
        both = dot(pick[...], jnp.concatenate([source[at], source[at + 1]], axis=0)).astype(BF16)
        last[i] = both[:48]
        first[i] = both[48:]


def edge_rows(level, from_left, from_right):
    pairs = (level.shape[0] + from_left.shape[0]) // 2
    return pl.pallas_call(
        edge_rows_body,
        out_shape=(jax.ShapeDtypeStruct(from_left.shape, BF16),)
        + (jax.ShapeDtypeStruct((pairs, 48, 128), BF16),) * 2,
        compiler_params=pltpu.CompilerParams(vmem_limit_bytes=8 * 1024 * 1024),
        name="edge_rows",
    )(level, from_left, from_right, jnp.asarray(edge_picks(), BF16))


def stencil_maps():
    ext = np.zeros((1, 224), np.int32)
    factor = np.zeros((2, 8, 224), np.float32)
    sign = np.zeros((4, 8))
    for q, (a, b) in enumerate(PAIRS):
        for h in range(2):
            sign[2 * q, a + 4 * h] = sign[2 * q, b + 4 * h] = 1.0
            sign[2 * q + 1, a + 4 * h] = 1.0
            sign[2 * q + 1, b + 4 * h] = -1.0
    for col in range(224):
        if col < 128:
            owner, child, ext[0, col] = (0, 1), col // 16, col % 16 + 3
        else:
            n = (col - 128) % 48
            owner, child = (n // 24,), n % 24 // 3
            ext[0, col] = n % 3 + (0 if col < 176 else 19)
        for parity in owner:
            for x in range(4):
                factor[parity, 2 * x, col] = sign[x, child]
                factor[parity, 2 * x + 1, col] = sign[x, child] * (1.0 if child >= 4 else -1.0)
    return ext, factor


def stencils_body(tap_u, weight_u, trig, tap_v, weight_v, ext, factor, polar, azimuth):
    rows = tap_u.shape[0]
    base = jnp.zeros((rows, ext.shape[1]), F32)
    for k in range(4):
        base = base + jnp.where(tap_u[:, k : k + 1] == ext[...], weight_u[:, k : k + 1], 0.0)
    for parity in range(2):
        for kind in range(8):
            turned = base * trig[:, kind % 2 : kind % 2 + 1]
            polar[parity, kind * rows : (kind + 1) * rows, :] = (
                turned * factor[parity, kind : kind + 1, :]
            ).astype(BF16)
    i = lax.broadcasted_iota(jnp.int32, (128, 128), 0)

    def fill(at, matrix, part, index):
        first = part == 0
        azimuth[index, at : at + 128, :128] = jnp.where(first, matrix, 0.0).astype(BF16)
        azimuth[index, at : at + 128, 128:] = jnp.where(first, 0.0, matrix).astype(BF16)

    def matrix_at(q):
        total = jnp.zeros((128, 128), F32)
        for k in range(4):
            total = total + jnp.where(tap_v[k : k + 1, :] == q, weight_v[k : k + 1, :], 0.0)
        return total

    own = matrix_at((i & 63) + 3)
    j = i & 3
    halo = jnp.where(j < 3, matrix_at(j + 67 * ((i >> 3) & 1)), 0.0)
    for index in range(8):
        fill(0, own, i >> 6, index)
        fill(128, jnp.where((i >> 4) == index, halo, 0.0), (i >> 2) & 1, index)


def stencils(tap_u, weight_u, trig, tap_v, weight_v):
    ext, factor = stencil_maps()
    rows = tap_u.shape[0]
    return pl.pallas_call(
        stencils_body,
        out_shape=(
            jax.ShapeDtypeStruct((2, 8 * rows, 224), BF16),
            jax.ShapeDtypeStruct((8, 256, 256), BF16),
        ),
        compiler_params=pltpu.CompilerParams(vmem_limit_bytes=8 * 1024 * 1024),
        name="stencils",
    )(tap_u, weight_u, trig, tap_v, weight_v, jnp.asarray(ext), jnp.asarray(factor))


def theta_stage(level, low, high, at, polar, half, swap):
    for i in range(level.shape[0] // 2):
        for parity in range(2):
            rhs = jnp.concatenate([level[2 * i + parity], low[at + i], high[at + i]], axis=0)
            y = dot(polar[parity], rhs)
            for x in range(4):
                c, s = y[64 * x : 64 * x + 32], y[64 * x + 32 : 64 * x + 64]
                half[2 * i + parity, 32 * x : 32 * x + 32] = (c + swap(s)).astype(BF16)


def top_body(
    src, off, order, starts, level, sides, low, high, polar, azimuth, tab, transfer, out,
    table, half, side_half, level4, sem,
):
    count = transfer.shape[0]
    fetch = pltpu.make_async_copy(transfer, table.at[pl.ds(0, count)], sem)
    fetch.start()
    table[count] = jnp.zeros(table.shape[1:], BF16)
    lane = lax.broadcasted_iota(jnp.int32, (32, 128), 1)
    wide = jnp.where(lane < 64, -1.0, 1.0)
    real = (lane & 4) == 0

    def swap_wide(s):
        return pltpu.roll(s, 64, 1) * wide

    def swap_near(s):
        return jnp.where(real, -pltpu.roll(s, 124, 1), pltpu.roll(s, 4, 1))

    theta_stage(level, low, high, 0, polar, half, swap_wide)
    theta_stage(sides, low, high, level.shape[0] // 2, polar, side_half, swap_near)

    def phi_stage(place, carry):
        rows = []
        for g in range(8):
            for x in range(4):
                a = slice(32 * x, 32 * x + 32)
                rows.append(jnp.concatenate([half[8 * g + place, a], side_half[g, a]], axis=1))
        y = dot(jnp.concatenate(rows, axis=0), azimuth[place])
        for g in range(8):
            re = im = None
            for q in range(2):
                at = 128 * g + 64 * q
                pr = y[at : at + 32, :128]
                pi = y[at : at + 32, 128:]
                qr = y[at + 32 : at + 64, :128]
                qi = y[at + 32 : at + 64, 128:]
                c = tab[2 * q]
                s = tab[2 * q + 1]
                dr = c * pr - s * qi
                di = c * pi + s * qr
                re, im = (dr, di) if q == 0 else (re + dr, im + di)
            at = pl.multiple_of((8 * g + place) * 64, 64)
            level4[pl.ds(at, 32), :] = re
            level4[pl.ds(at + 32, 32), :] = im
        return carry

    lax.fori_loop(0, 8, phi_stage, 0)
    fetch.wait()
    targets = out.shape[0]
    slots = src.shape[0] // targets

    def one(t, count):
        re = [jnp.zeros((8, 128), F32)] * 4
        im = [jnp.zeros((8, 128), F32)] * 4
        for j in range(count):
            at = pl.multiple_of(src[t * slots + j], 64)
            w = table.at[off[t * slots + j]]
            for r in range(4):
                xr = level4[pl.ds(at + 8 * r, 8), :]
                xi = level4[pl.ds(at + 32 + 8 * r, 8), :]
                wr = w[0, 8 * r : 8 * r + 8].astype(F32)
                wi = w[1, 8 * r : 8 * r + 8].astype(F32)
                re[r] = re[r] + (wr * xr - wi * xi)
                im[r] = im[r] + (wr * xi + wi * xr)
        for r in range(4):
            out[t, 0, 8 * r : 8 * r + 8] = re[r].astype(BF16)
            out[t, 1, 8 * r : 8 * r + 8] = im[r].astype(BF16)

    by_class(order, starts, slots, 2, one)


def top_level(level, sides, low, high, polar, azimuth, tab, transfer, lists):
    count, _, rows, cols = transfer.shape
    parents = level.shape[0]
    lines = (polar.shape[1] // 2, level.shape[2])
    return pl.pallas_call(
        top_body,
        in_specs=[SMEM_SPEC] * 4 + [VMEM_SPEC] * 7 + [ANY_SPEC],
        out_specs=VMEM_SPEC,
        out_shape=jax.ShapeDtypeStruct((parents, 2, rows, cols), BF16),
        scratch_shapes=[
            pltpu.VMEM((count + 1, 2, rows, cols), BF16),
            pltpu.VMEM((parents,) + lines, BF16),
            pltpu.VMEM((sides.shape[0],) + lines, BF16),
            pltpu.VMEM((parents * 2 * rows, cols), F32),
            pltpu.SemaphoreType.DMA,
        ],
        compiler_params=pltpu.CompilerParams(vmem_limit_bytes=30 * 1024 * 1024),
        name="top_level",
    )(*lists, level, sides, low, high, polar, azimuth, tab, transfer)


def flat_lists(sources, offsets, dead, source_rows, factor_rows):
    src = jnp.maximum(sources, 0) * source_rows
    off = jnp.where(offsets < 0, dead, offsets) * factor_rows
    return (src.reshape(-1), off.reshape(-1)) + target_classes(sources)


def shards(
    patterns7,
    polar_up7,
    azimuth_up7,
    polar_up6,
    azimuth_up6,
    polar_first,
    polar_weights,
    azimuth_first,
    azimuth_weights,
    transfer5,
    sources5,
    offsets5,
    transfer4,
    sources4,
    offsets4,
):
    bands = lax.axis_size("ang")
    blocks = lax.axis_size("clu")
    band = lax.axis_index("ang")
    block = lax.axis_index("clu")

    send = aggregate(patterns7, polar_up7, azimuth_up7, polar_up6, azimuth_up6)
    arrived = lax.all_to_all(send, ("clu", "ang"), split_axis=0, concat_axis=0, tiled=True)

    count5 = transfer5.shape[0]
    count4 = transfer4.shape[0]
    table5 = transfer_table(transfer5)
    half5 = sources5.shape[0] // 2
    lists5 = (
        flat_lists(sources5[:half5], offsets5[:half5], count5, 16, 16),
        flat_lists(sources5[half5:], offsets5[half5:], count5, 16, 16),
    )
    lists4 = flat_lists(sources4, offsets4, count4, 64, 1)
    rows4 = polar_first.shape[0]
    cols4 = azimuth_first.shape[0]
    band_rows = rows4 // bands
    block_cols = cols4 // blocks
    taps = jnp.arange(4, dtype=jnp.int32)
    tap_u = lax.dynamic_slice_in_dim(polar_first, band * band_rows, band_rows, 0)
    tap_u = (tap_u - band * (band_rows // 2) + 3)[:, None] + taps[None, :]
    weight_u = lax.dynamic_slice_in_dim(polar_weights, band * band_rows, band_rows, 0).astype(F32)
    tap_v = lax.dynamic_slice_in_dim(azimuth_first, block * block_cols, block_cols, 0)
    tap_v = (tap_v[None, :] + taps[:, None] - block * (block_cols // 2) + 3) % (cols4 // 2)
    weight_v = lax.dynamic_slice_in_dim(azimuth_weights, block * block_cols, block_cols, 0)
    weight_v = weight_v.T.astype(F32)
    theta = (jnp.arange(band_rows, dtype=jnp.int32) + band * band_rows).astype(F32)
    theta = (theta + 0.5) * (math.pi / rows4)
    phi = (jnp.arange(block_cols, dtype=jnp.int32) + block * block_cols).astype(F32)
    phi = phi * (2.0 * math.pi / cols4)
    scale = rows4 / 8.0
    lift = scale * jnp.cos(theta)
    trig = jnp.stack([jnp.cos(lift), jnp.sin(lift)], axis=1)
    x = jnp.sin(theta)[:, None] * jnp.cos(phi)[None, :]
    y = jnp.sin(theta)[:, None] * jnp.sin(phi)[None, :]
    f0 = scale * (x + y)
    f1 = scale * (x - y)
    tab = jnp.stack([jnp.cos(f0), jnp.sin(f0), jnp.cos(f1), jnp.sin(f1)])
    polar, azimuth = stencils(tap_u, weight_u, trig, tap_v, weight_v)
    arrived, table5, lists5, lists4, polar, azimuth, tab = lax.optimization_barrier(
        (arrived, table5, lists5, lists4, polar, azimuth, tab)
    )

    level = arrived.reshape(64, 128, 128)
    right, left = edge_columns(level)
    around = lambda step: [(i, (i + step) % blocks) for i in range(blocks)]
    across = lambda step: [(i, i + step) for i in range(bands) if 0 <= i + step < bands]
    from_left = lax.ppermute(right, "clu", around(1))
    from_right = lax.ppermute(left, "clu", around(-1))
    before, tiles, table5 = translate_first(arrived.reshape(512, 16, 128), table5, lists5[0])
    from_left, from_right, tiles = lax.optimization_barrier((from_left, from_right, tiles))
    sides, last, first = edge_rows(level, from_left, from_right)
    last, first, tiles = lax.optimization_barrier((last, first, tiles))
    low = lax.ppermute(last, "ang", across(1))
    high = lax.ppermute(first, "ang", across(-1))
    translated5 = translate_last(tiles, table5, before, lists5[1])
    translated4 = top_level(
        level, sides, low, high, polar, azimuth, tab, transfer4, lists4
    )
    return (translated5, translated4)


def solution(mesh):
    in_specs = (
        P(("clu", "ang"), None, None, None),
        P(),
        P(),
        P(),
        P(),
        P(),
        P(),
        P(),
        P(),
        P(None, None, "ang", "clu"),
        P(),
        P(),
        P(None, None, "ang", "clu"),
        P(),
        P(),
    )
    out_specs = (P(None, None, "ang", "clu"), P(None, None, "ang", "clu"))
    return jax.shard_map(shards, mesh=mesh, in_specs=in_specs, out_specs=out_specs, check_vma=False)
```
